128 devices in a mesh: px: 8 (over y, core), py: 16 (over x, z).
Axes of the slice: x: 4, y: 4, z: 4, core: 2. Of those that a mesh axis runs over, the one named last changes fastest.
Arguments:
- parent_field: float32 [192, 384, 640], P('px', 'py'), may hold values from -6 to 6
- nest_field: float32 [192, 384, 640], P('px', 'py'), may hold values from -6 to 6
- anchor: int32 [2], replicated, may hold values from 1 to 125, as said below
- displacement: int32 [2], replicated, may hold values from 1 to 2, as said below
- feedback_weight: float32 [640], replicated, may hold values from 0.3 to 0.9
- rim_weight: float32 [3], replicated, may hold values from 0.3 to 1
Outputs:
- parent_new: float32 [192, 384, 640], P('px', 'py')
- nest_new: float32 [192, 384, 640], P('px', 'py')
The draws below stay inside these ranges and needn't reach their ends.
Inputs may be any that keep to these rules, and one draw needn't show every extreme that they name: `displacement`: at least one of the two entries equals 2. `anchor`: the two entries differ; one of them equals the largest value.
All inputs are finite; a program needn't handle non-finite values.
Results may differ from the reference program's by a relative error of at most 0.000067.
Values sent between devices are 32-bit elements; how exact they have to be, the bound alone decides.
A program may use at most 128 MiB of HBM per device.

```python
import jax
import jax.numpy as jnp
from jax import lax

CHAN = 640
REFINE = 3
MAX_MOVE = 2
RIM_CELLS = 3
NEST_NX = 192
NEST_NY = 384
PAR_NX = 192
PAR_NY = 384


def draw_displacement(key, part):
    first_key, second_key = jax.random.split(jax.random.fold_in(key, 17))
    other = jax.random.randint(first_key, (), 1, MAX_MOVE + 1)
    flip = jax.random.randint(second_key, (), 0, 2)
    largest = jnp.int32(MAX_MOVE)
    first_entry = jnp.where(flip == 0, largest, other)
    second_entry = jnp.where(flip == 0, other, largest)
    return jnp.stack([first_entry, second_entry]).astype(jnp.int32)


def draw_anchor(key, part):
    first_key, second_key = jax.random.split(jax.random.fold_in(key, 29))
    top_value = min(PAR_NX - NEST_NX // REFINE, PAR_NY - NEST_NY // REFINE) - MAX_MOVE - 1
    other = jax.random.randint(first_key, (), 1, top_value)
    flip = jax.random.randint(second_key, (), 0, 2)
    largest = jnp.int32(top_value)
    first_entry = jnp.where(flip == 0, largest, other)
    second_entry = jnp.where(flip == 0, other, largest)
    return jnp.stack([first_entry, second_entry]).astype(jnp.int32)


def level_of(rng, dims, pieces, low, high):
    loudness, own = 1.0, jax.random.fold_in(rng, 6)
    for dim, blocks in pieces:
        draws = jnp.exp(jax.random.uniform(jax.random.fold_in(own, dim), (blocks,), jnp.float32, low / len(pieces), high / len(pieces)))
        loudness = loudness * jnp.repeat(draws, dims[dim] // blocks).reshape([-1 if axis == dim else 1 for axis in range(len(dims))])
    return loudness


def normal_values(own_key, extent, width, most, pieces=(), dtype=jnp.bfloat16):
    level = level_of(own_key, extent, pieces, -0.22, 0.18) if pieces else 1.0
    values = jax.random.normal(own_key, extent, jnp.float32) * width * level
    return jnp.minimum(jnp.maximum(values, -most), most).astype(dtype)


def setup_inputs(seed: int = 0) -> dict:
    streams_of = jax.random.split(jax.random.key(seed), 7)
    parent_field = normal_values(streams_of[0], (PAR_NX, PAR_NY, CHAN), 1.0, 6.0, ((0, 8), (1, 16)), jnp.float32)
    nest_field = normal_values(streams_of[1], (NEST_NX, NEST_NY, CHAN), 1.0, 6.0, ((0, 8), (1, 16)), jnp.float32)
    anchor = draw_anchor(jax.random.fold_in(streams_of[6], 71), 0)
    displacement = draw_displacement(jax.random.fold_in(streams_of[6], 71), 0)
    feedback_weight = jnp.clip(jax.random.uniform(streams_of[4], (CHAN,), jnp.float32, 0.3, 0.9), 0.3, 0.9)
    rim_weight = jnp.clip(jax.random.uniform(streams_of[5], (RIM_CELLS,), jnp.float32, 0.3, 1.0), 0.3, 1.0)
    return dict(parent_field=parent_field, nest_field=nest_field, anchor=anchor, displacement=displacement, feedback_weight=feedback_weight, rim_weight=rim_weight)


def interp_matrix(rows_total, window_rows):
    row_ids = jnp.arange(rows_total)
    coarse = (row_ids // REFINE)[:, None]
    frac = ((row_ids % REFINE).astype(jnp.float32) + 0.5) / REFINE - 0.5
    frac = frac[:, None]
    columns = jnp.arange(window_rows)[None, :]
    low_side = frac < 0
    weight_left = jnp.where(low_side, -frac, 0.0)
    weight_mid = jnp.where(low_side, 1.0 + frac, 1.0 - frac)
    weight_right = jnp.where(low_side, 0.0, frac)
    result = jnp.where(columns == coarse, weight_left, 0.0)
    result = result + jnp.where(columns == coarse + 1, weight_mid, 0.0)
    result = result + jnp.where(columns == coarse + 2, weight_right, 0.0)
    return result.astype(jnp.float32)


def rim_blend(distance, rim_weight):
    blend = jnp.zeros(distance.shape, jnp.float32)
    for level in range(RIM_CELLS):
        blend = blend + jnp.where(distance == level, rim_weight[level], 0.0)
    return blend


def reference(parent_field, nest_field, anchor, displacement, feedback_weight, rim_weight):
    nest_nx = nest_field.shape[0]
    nest_ny = nest_field.shape[1]
    foot_x = nest_nx // REFINE
    foot_y = nest_ny // REFINE
    chan = parent_field.shape[2]
    shift_x = displacement[0]
    shift_y = displacement[1]
    corner_x = (anchor[0] + shift_x).astype(jnp.int32)
    corner_y = (anchor[1] + shift_y).astype(jnp.int32)
    zero_index = jnp.int32(0)
    window = lax.dynamic_slice(parent_field, (corner_x - 1, corner_y - 1, zero_index), (foot_x + 2, foot_y + 2, chan))
    weights_x = interp_matrix(nest_nx, foot_x + 2)
    weights_y = interp_matrix(nest_ny, foot_y + 2)
    inner_sum = jnp.einsum("jy,xyc->xjc", weights_y, window, precision=lax.Precision.HIGHEST)
    interp = jnp.einsum("ix,xjc->ijc", weights_x, inner_sum, precision=lax.Precision.HIGHEST)
    margin = REFINE * MAX_MOVE
    padded = jnp.pad(nest_field, ((0, margin), (0, margin), (0, 0)))
    shifted = lax.dynamic_slice(padded, ((REFINE * shift_x).astype(jnp.int32), (REFINE * shift_y).astype(jnp.int32), zero_index), nest_field.shape)
    rows_global = jnp.arange(nest_nx)[:, None, None]
    cols_global = jnp.arange(nest_ny)[None, :, None]
    newly_entered = (rows_global + REFINE * shift_x >= nest_nx) | (cols_global + REFINE * shift_y >= nest_ny)
    moved = jnp.where(newly_entered, interp, shifted)
    distance = jnp.minimum(jnp.minimum(rows_global, cols_global), jnp.minimum(nest_nx - 1 - rows_global, nest_ny - 1 - cols_global))
    blend = rim_blend(distance, rim_weight)
    nest_new = moved + blend * (interp - moved)
    average = nest_new.reshape(foot_x, REFINE, foot_y, REFINE, chan).sum(axis=(1, 3)) * (1.0 / (REFINE * REFINE))
    region = lax.dynamic_slice(parent_field, (corner_x, corner_y, zero_index), (foot_x, foot_y, chan))
    updated = region + feedback_weight * (average - region)
    parent_new = lax.dynamic_update_slice(parent_field, updated, (corner_x, corner_y, zero_index))
    return parent_new, nest_new
```

```python
import functools

import jax
import jax.numpy as jnp
from jax import lax
from jax.experimental import pallas as pl
from jax.experimental.pallas import tpu as pltpu
from jax.sharding import PartitionSpec as P

REFINE = 3
TILE = 24
BLOCK = 8
LANES = 128
CHUNKS = 5
CHAN = CHUNKS * LANES
RIM_CELLS = 3
MARGIN = 2 * REFINE
NX, NY = 8, 16
FOOT_X, FOOT_Y = NX * BLOCK, NY * BLOCK
FINE_X, FINE_Y = NX * TILE, NY * TILE
PAD = 16
WINDOW_ORDER = ((0, 0), (0, 1), (0, 2), (1, 1), (1, 2))
TOP = 125
MESH = pl.DeviceIdType.MESH
TAPS = ((1 / 3, 2 / 3, 0.0), (0.0, 1.0, 0.0), (0.0, 2 / 3, 1 / 3))


def combine(taps, values):
    total = None
    for tap, value in zip(taps, values):
        if tap == 0.0:
            continue
        term = value if tap == 1.0 else tap * value
        total = term if total is None else total + term
    return total


class Dim:
    def __init__(self, count, q, low, high):
        self.count, self.q, self.low, self.high = count, q, low, high
        self.fixed = low == high
        self.second_from = 2 if BLOCK + high + 1 + 9 < TILE else 1
        first, last = BLOCK * q + low, BLOCK * q + high + 1
        self.near = sorted({first // TILE, (last + 2) // TILE})
        far = BLOCK * (count - 1) + 6
        self.far = sorted({(first + far) // TILE, (last + far + 3) // TILE})

    def pieces(self, index):
        g = index + self.q
        owner, phase = lax.div(g, 3), lax.rem(g, 3)
        if self.fixed:
            cut = BLOCK - self.low
            return (
                (phase < 2, owner, phase + 1, 0, BLOCK),
                (phase == 2, owner, phase + 1, 0, cut),
                (phase == 2, owner + 1, 0, cut, BLOCK - cut),
            )
        return ((phase < 3, owner, phase + 1, 0, BLOCK), (phase == 2, owner + 1, 0, 0, BLOCK))

    def slots(self, index):
        found = []
        for slot in range(4):
            source = 3 * index - 1 + slot - self.q
            start, size = 0, BLOCK
            if self.fixed and slot == 0:
                start, size = BLOCK - self.low, self.low
            if self.fixed and slot == 3:
                start, size = 0, BLOCK - self.low
            found.append(((source >= 0) & (source < self.count), source, start, size))
        return found

    def window_targets(self, index):
        found = []
        for order, (second, phase) in enumerate(WINDOW_ORDER):
            if second and phase < self.second_from:
                continue
            target = 3 * (index - second) + phase - self.q
            found.append((order, (target >= 0) & (target < self.count), target, second))
        return found

    def window_owners(self, index):
        g = index + self.q
        owner, phase = lax.div(g, 3), lax.rem(g, 3)
        return (
            (phase < 3, owner, 0),
            ((phase >= self.second_from) & (owner + 1 < self.count), owner + 1, 1),
        )

    def strip_role(self, index):
        near, either, place = jnp.bool_(False), jnp.bool_(False), jnp.int32(0)
        for owners in (self.near, self.far):
            for order, owner in enumerate(owners):
                hit = index == owner
                either = either | hit
                if owners is self.near:
                    near = near | hit
                if order:
                    place = jnp.where(hit, order, place)
        return near, either, place


def send_kernel(
    dim_x, dim_y,
    nest, parent, average, send_x, send_y,
    arrived, nest_below, nest_beside, nest_corner, halo_rows, halo_cols, halo_corners, recv_x, recv_y,
    avg_send, avg_recv, nest_send, nest_recv, par_send, par_recv, wx_send, wx_recv, wy_send, wy_recv,
):
    me_x, me_y = lax.axis_index("px"), lax.axis_index("py")
    sends, receives = [], []
    pieces = [(a, b) for a in dim_x.pieces(me_x) for b in dim_y.pieces(me_y)]
    for order, ((has_x, own_x, slot_x, from_x, size_x), (has_y, own_y, slot_y, from_y, size_y)) in enumerate(pieces):
        sends.append((
            has_x & has_y, own_x, own_y,
            average.at[pl.ds(from_x, size_x), pl.ds(from_y, size_y), :],
            arrived.at[slot_x, slot_y, pl.ds(from_x, size_x), pl.ds(from_y, size_y), :],
            avg_send.at[order], avg_recv.at[slot_x, slot_y], True,
        ))
    for slot_x, (has_x, src_x, from_x, size_x) in enumerate(dim_x.slots(me_x)):
        for slot_y, (has_y, src_y, from_y, size_y) in enumerate(dim_y.slots(me_y)):
            receives.append((
                has_x & has_y, src_x, src_y,
                arrived.at[slot_x, slot_y, pl.ds(from_x, size_x), pl.ds(from_y, size_y), :],
                avg_recv.at[slot_x, slot_y],
            ))
    for order, (step_x, step_y) in enumerate(((1, 0), (0, 1), (1, 1))):
        rows, cols = (MARGIN if step_x else TILE), (MARGIN if step_y else TILE)
        lands = (nest_below, nest_beside, nest_corner)[order].at[:, pl.ds(0, cols), :]
        sends.append((
            (me_x >= step_x) & (me_y >= step_y), me_x - step_x, me_y - step_y,
            nest.at[pl.ds(0, rows), pl.ds(0, cols), :], lands, nest_send.at[order], nest_recv.at[order], False,
        ))
        receives.append((
            (me_x + step_x < NX) & (me_y + step_y < NY), me_x + step_x, me_y + step_y, lands, nest_recv.at[order],
        ))
    for order, (step_x, step_y) in enumerate([(a, b) for a in (-1, 0, 1) for b in (-1, 0, 1) if a or b]):
        span = {-1: pl.ds(0, 1), 0: pl.ds(0, TILE), 1: pl.ds(TILE - 1, 1)}
        side_x, side_y = int(step_x < 0), int(step_y < 0)
        if step_y == 0:
            lands = halo_rows.at[side_x]
        elif step_x == 0:
            lands = halo_cols.at[:, pl.ds(side_y, 1), :]
        else:
            lands = halo_corners.at[side_x, pl.ds(0, 1), pl.ds(side_y, 1), :]
        source = parent.at[span[step_x], span[step_y], :]
        if step_y == 0:
            source = parent.at[0 if step_x < 0 else TILE - 1]
        to_x, to_y, from_x, from_y = me_x + step_x, me_y + step_y, me_x - step_x, me_y - step_y
        sends.append((
            (to_x >= 0) & (to_x < NX) & (to_y >= 0) & (to_y < NY), to_x, to_y,
            source, lands, par_send.at[order], par_recv.at[order], False,
        ))
        receives.append((
            (from_x >= 0) & (from_x < NX) & (from_y >= 0) & (from_y < NY), from_x, from_y, lands, par_recv.at[order],
        ))
    near_x, strip_x, place_x = dim_x.strip_role(me_x)
    near_y, strip_y, place_y = dim_y.strip_role(me_y)
    for order, has, target, second in dim_y.window_targets(me_y):
        sends.append((
            strip_x & has, jnp.where(near_x, 0, NX - 1), target,
            send_x.at[order, :], recv_x.at[place_x, second, :],
            wx_send.at[order], wx_recv.at[place_x, second], True,
        ))
    for order, has, target, second in dim_x.window_targets(me_x):
        sends.append((
            strip_y & has, target, jnp.where(near_y, 0, NY - 1),
            send_y.at[order, :, pl.ds(0, 4), :], recv_y.at[place_y, second, :, pl.ds(0, 4), :],
            wy_send.at[order], wy_recv.at[place_y, second], True,
        ))
    for dim, index, along, me_along in ((dim_x, me_x, dim_y, me_y), (dim_y, me_y, dim_x, me_x)):
        for place in range(max(len(dim.near), len(dim.far))):
            here_near = dim.near[place] if place < len(dim.near) else -1
            here_far = dim.far[place] if place < len(dim.far) else -1
            across = jnp.where(index == 0, here_near, here_far)
            for has, owner, second in along.window_owners(me_along):
                cond = ((index == 0) | (index == dim.count - 1)) & (across >= 0) & has
                if dim is dim_x:
                    receives.append((cond, across, owner, recv_x.at[place, second, :], wx_recv.at[place, second]))
                else:
                    receives.append((cond, owner, across, recv_y.at[place, second, :, pl.ds(0, 4), :], wy_recv.at[place, second]))

    barrier = pltpu.get_barrier_semaphore()
    for has, src_x, src_y, _, _ in receives:
        @pl.when(has & ((src_x != me_x) | (src_y != me_y)))
        def _():
            pl.semaphore_signal(barrier, inc=1, device_id=(src_x, src_y), device_id_type=MESH)

    expected = jnp.int32(0)
    for has, to_x, to_y, *_ in sends:
        expected = expected + jnp.where(has & ((to_x != me_x) | (to_y != me_y)), 1, 0)
    pl.semaphore_wait(barrier, expected)

    def remote(entry):
        _, to_x, to_y, src, dst, send_sem, recv_sem, _ = entry
        return pltpu.make_async_remote_copy(
            src_ref=src, dst_ref=dst, send_sem=send_sem, recv_sem=recv_sem, device_id=(to_x, to_y), device_id_type=MESH)

    for entry in sends:
        has, to_x, to_y, src, dst, _, recv_sem, maybe_self = entry
        own = (to_x == me_x) & (to_y == me_y)

        @pl.when(has & jnp.logical_not(own))
        def _():
            remote(entry).start()

        if maybe_self:
            @pl.when(has & own)
            def _():
                pltpu.make_async_copy(src, dst, recv_sem).start()

    for has, _, _, dst, recv_sem in receives:
        @pl.when(has)
        def _():
            pltpu.make_async_copy(dst, dst, recv_sem).wait()

    for entry in sends:
        has, to_x, to_y, *_ = entry

        @pl.when(has & ((to_x != me_x) | (to_y != me_y)))
        def _():
            remote(entry).wait_send()


CROSSED = (
    (4, 4, BLOCK, BLOCK), (MARGIN, TILE), (TILE, 8), (MARGIN, 8), (2, TILE), (TILE, 8), (2, 1, 8), (2, 2, 4, 16), (2, 2, 10, 8),
)


def free(count, q):
    return Dim(count, q, max(0, 1 - BLOCK * q), min(BLOCK - 1, TOP - 1 - BLOCK * q))


def variant(order):
    if order < 16:
        dims = Dim(NX, TOP // BLOCK, TOP % BLOCK, TOP % BLOCK), free(NY, order)
    else:
        dims = free(NX, order - 16), Dim(NY, TOP // BLOCK, TOP % BLOCK, TOP % BLOCK)
    dma = pltpu.SemaphoreType.DMA
    hbm = pl.BlockSpec(memory_space=pl.ANY)
    return pl.pallas_call(
        functools.partial(send_kernel, *dims),
        name=f"send_{order}",
        out_shape=tuple(jax.ShapeDtypeStruct((*dims, CHAN), jnp.float32) for dims in CROSSED),
        in_specs=[hbm] * 5,
        out_specs=(hbm,) * len(CROSSED),
        scratch_shapes=[
            dma((9,)), dma((4, 4)), dma((3,)), dma((3,)), dma((8,)), dma((8,)),
            dma((5,)), dma((2, 2)), dma((5,)), dma((2, 2)),
        ],
        compiler_params=pltpu.CompilerParams(collective_id=order, has_side_effects=True),
    )


def facts_of(anchor_ref, move_ref):
    move = move_ref[0], move_ref[1]
    anchor = anchor_ref[0], anchor_ref[1]
    corner = anchor[0] + move[0], anchor[1] + move[1]
    q = lax.div(anchor[0], BLOCK), lax.div(anchor[1], BLOCK)
    phase = anchor[0] - BLOCK * q[0], anchor[1] - BLOCK * q[1]
    return move, corner, q, phase


def blender(rim_ref):
    rims = [rim_ref[level] for level in range(RIM_CELLS)]

    def blend_of(distance):
        value = jnp.where(distance == 2, rims[2], 0.0)
        value = jnp.where(distance == 1, rims[1], value)
        return jnp.where(distance == 0, rims[0], value)

    return blend_of


def iota(rows):
    return lax.broadcasted_iota(jnp.int32, (rows, LANES), 0)


def prepare_kernel(anchor_ref, move_ref, rim_ref, nest, parent, average, send_x, send_y, padded):
    me_x, me_y = lax.axis_index("px"), lax.axis_index("py")
    (move_x, move_y), (corner_x, corner_y), _, (phase_x, phase_y) = facts_of(anchor_ref, move_ref)
    blend_of = blender(rim_ref)

    @pl.loop(0, BLOCK)
    def _(k):
        row = REFINE * (BLOCK * me_x + k - move_x)
        col = REFINE * (BLOCK * me_y + iota(BLOCK) - move_y)
        total = None
        for ii in range(3):
            for jj in range(3):
                keep = (1.0 - blend_of(jnp.minimum(col + jj, row + ii))) * (1.0 / 9.0)
                term = keep * nest[REFINE * k + ii, pl.ds(jj, BLOCK, stride=REFINE), :]
                total = term if total is None else total + term
        average[k] = total

    def strip(corner, foot, me):
        first = corner - 1 - TILE * me
        near = (first <= TILE - 1) & (first + 2 >= 0)
        far = (first + foot - 2 <= TILE - 1) & (first + foot + 1 >= 0)
        return near | far, first + jnp.where(near, 0, foot - 2)

    strip_x, first_row = strip(corner_x, FOOT_X, me_x)
    strip_y, first_col = strip(corner_y, FOOT_Y, me_y)

    @pl.when(strip_x | strip_y)
    def _():
        @pl.loop(0, TILE)
        def _(row):
            padded[row, pl.ds(PAD, TILE), :] = parent[row]

    @pl.when(strip_x)
    def _():
        for order, (second, phase) in enumerate(WINDOW_ORDER):
            start = PAD + BLOCK * phase - TILE * second + phase_y + move_y - 1
            for m in range(4):
                send_x[order, m] = padded[jnp.clip(first_row + m, 0, TILE - 1), pl.ds(jnp.clip(start, 0, TILE + PAD), 16, stride=1), :]

    @pl.when(strip_y)
    def _():
        for order, (second, phase) in enumerate(WINDOW_ORDER):
            first = BLOCK * phase - TILE * second + phase_x + move_x - 1
            for m in range(10):
                send_y[order, m] = padded[jnp.clip(first + m, 0, TILE - 1), pl.ds(jnp.clip(PAD + first_col, 0, TILE + PAD), 8, stride=1), :]


def finish_kernel(
    anchor_ref, move_ref, rim_ref,
    parent, nest, feed, arrived, nest_below, nest_beside, nest_corner, halo_rows, halo_cols, halo_corners, recv_x, recv_y,
    parent_new, nest_new,
    wide_nest, wide_parent, placed, coefs, merged_x, fine_x, merged_y, fine_y,
):
    me_x, me_y = lax.axis_index("px"), lax.axis_index("py")
    (move_x, move_y), (corner_x, corner_y), (q_x, q_y), (phase_x, phase_y) = facts_of(anchor_ref, move_ref)
    blend_of = blender(rim_ref)

    @pl.loop(0, TILE)
    def _(row):
        wide_nest[row, pl.ds(0, TILE), :] = nest[row]
        wide_nest[row, pl.ds(TILE, 8), :] = nest_beside[row]

    @pl.loop(0, MARGIN)
    def _(row):
        wide_nest[TILE + row, pl.ds(0, TILE), :] = nest_below[row]
        wide_nest[TILE + row, pl.ds(TILE, 8), :] = nest_corner[row]

    @pl.loop(0, TILE)
    def _(row):
        nest_new[row] = wide_nest[row + REFINE * move_x, pl.ds(REFINE * move_y, TILE, stride=1), :]

    def blended(row, cols, shifted, interp):
        entered = (cols >= FINE_Y - REFINE * move_y) | (cols * 0 + row >= FINE_X - REFINE * move_x)
        moved = jnp.where(entered, interp, shifted)
        distance = jnp.minimum(jnp.minimum(cols, FINE_Y - 1 - cols), jnp.minimum(row, FINE_X - 1 - row))
        return moved + blend_of(distance) * (interp - moved)

    def edge_columns(at_near):
        rel_row = BLOCK * lax.rem(me_x + q_x, 3) + phase_x + move_x - 1
        columns = iota(BLOCK)
        if at_near:
            first_col, step, bound, base = 0, columns, TILE * (lax.div(q_y, 3) + 1), corner_y - 1
        else:
            first_col, step = TILE - BLOCK, columns - 2
            bound, base = TILE * (lax.div(q_y + NY - 1, 3) + 1), corner_y - 1 + FOOT_Y - 2
        beyond = base + columns >= bound
        cell = jnp.where(step >= 3, 1, 0)
        sub = step - 3 * cell
        taps = []
        for n in range(3 if at_near else 4):
            m = n - cell
            left = jnp.where(m == 0, 1 / 3, jnp.where(m == 1, 2 / 3, 0.0))
            mid = jnp.where(m == 1, 1.0, 0.0)
            right = jnp.where(m == 1, 2 / 3, jnp.where(m == 2, 1 / 3, 0.0))
            taps.append(jnp.where(sub == 0, left, jnp.where(sub == 1, mid, right)))
        in_strip = (step >= 0) & (step < (3 if at_near else 6))
        for m in range(10):
            second = jnp.where(rel_row + m >= TILE, 1, 0)
            merged_y[m] = jnp.where(beyond, recv_y[1, second, m], recv_y[0, second, m])
            total = None
            for n, tap in enumerate(taps):
                term = tap * jnp.broadcast_to(merged_y[m, n:n + 1, :], (BLOCK, LANES))
                total = term if total is None else total + term
            fine_y[m] = total

        @pl.loop(0, BLOCK)
        def _(k):
            for ii in range(3):
                row = REFINE * k + ii
                interp = combine(TAPS[ii], [fine_y[k + m] for m in range(3)])
                shifted = wide_nest[row + REFINE * move_x, pl.ds(first_col + REFINE * move_y, BLOCK, stride=1), :]
                value = blended(TILE * me_x + row, TILE * me_y + first_col + columns, shifted, interp)
                nest_new[row, pl.ds(first_col, BLOCK), :] = jnp.where(in_strip, value, shifted)

    def edge_rows(at_near):
        rel_col = BLOCK * lax.rem(me_y + q_y, 3) + phase_y + move_y - 1
        second = rel_col + iota(16) >= TILE
        cols = TILE * me_y + iota(TILE)
        if at_near:
            bound, first_row, cells = TILE * (lax.div(q_x, 3) + 1), corner_x - 1, 1
        else:
            bound, first_row, cells = TILE * (lax.div(q_x + NX - 1, 3) + 1), corner_x - 1 + FOOT_X - 2, 2
        for m in range(cells + 2):
            place = jnp.where(first_row + m >= bound, 1, 0)
            merged_x[...] = jnp.where(second, recv_x[place, 1, m], recv_x[place, 0, m])
            for jj in range(3):
                fine_x[m, pl.ds(jj, BLOCK, stride=REFINE), :] = combine(
                    TAPS[jj], [merged_x[pl.ds(n, BLOCK), :] for n in range(3)])
        for k in range(cells):
            for ii in range(3):
                row = (0 if at_near else TILE - 3 * cells) + 3 * k + ii
                interp = combine(TAPS[ii], [fine_x[k + m] for m in range(3)])
                shifted = wide_nest[row + REFINE * move_x, pl.ds(REFINE * move_y, TILE, stride=1), :]
                nest_new[row] = blended(TILE * me_x + row, cols, shifted, interp)

    for at_near in (True, False):
        @pl.when(me_y == (0 if at_near else NY - 1))
        def _():
            edge_columns(at_near)
    for at_near in (True, False):
        @pl.when(me_x == (0 if at_near else NX - 1))
        def _():
            edge_rows(at_near)

    first_k, first_l = TILE * me_x - corner_x, TILE * me_y - corner_y
    touched = (first_k < FOOT_X) & (first_k + TILE > 0) & (first_l < FOOT_Y) & (first_l + TILE > 0)

    @pl.when(jnp.logical_not(touched))
    def _():
        parent_new[...] = parent[...]

    @pl.when(touched)
    def _():
        l = first_l + iota(TILE)
        weight = feed[...]

        @pl.loop(0, TILE)
        def _(row):
            k = l * 0 + (first_k + row)
            covered = (l >= 0) & (l < FOOT_Y) & (k >= 0) & (k < FOOT_X)
            usable = covered & (l < FOOT_Y - move_y) & (k < FOOT_X - move_x)
            at = row + BLOCK - phase_x
            slot_x, in_x = lax.div(at, BLOCK), lax.rem(at, BLOCK)
            whole = jnp.concatenate([arrived[slot_x, slot_y, in_x] for slot_y in range(4)], axis=0)
            whole = pltpu.roll(whole, 3 * BLOCK + phase_y, 0)[:TILE]
            whole = jnp.where(usable, whole, 0.0)
            own = parent[row]
            placed[row] = whole
            parent_new[row] = jnp.where(covered, own + weight * (whole - own), own)

        near_row = (first_k <= 0) & (first_k + TILE > 0)
        near_col = (first_l <= 0) & (first_l + TILE > 0)
        far_row = (first_k < FOOT_X) & (first_k + TILE > FOOT_X - move_x)
        far_col = (first_l < FOOT_Y) & (first_l + TILE > FOOT_Y - move_y)

        @pl.when(near_row | near_col | far_row | far_col)
        def _():
            @pl.loop(0, TILE)
            def _(row):
                wide_parent[row + 1, pl.ds(8, TILE), :] = parent[row]
                wide_parent[row + 1, pl.ds(7, 1), :] = halo_cols[row, 0:1, :]
                wide_parent[row + 1, pl.ds(8 + TILE, 1), :] = halo_cols[row, 1:2, :]

            for side, row in ((0, 0), (1, TILE + 1)):
                wide_parent[row, pl.ds(8, TILE), :] = halo_rows[side]
                wide_parent[row, pl.ds(7, 1), :] = halo_corners[side, 0, 0:1, :]
                wide_parent[row, pl.ds(8 + TILE, 1), :] = halo_corners[side, 0, 1:2, :]

            def fix(row, tile, place):
                cols = first_l + BLOCK * tile + iota(BLOCK)
                k = first_k + row

                @pl.when(pl.program_id(0) == 0)
                def _():
                    entered = (cols >= FOOT_Y - move_y) | (cols * 0 + k >= FOOT_X - move_x)
                    partial = []
                    for ii in range(3):
                        weights = [
                            jnp.where(entered, 1.0, blend_of(jnp.minimum(REFINE * cols + jj, REFINE * k + ii)))
                            for jj in range(3)
                        ]
                        partial.append([combine([TAPS[jj][n] for jj in range(3)], weights) for n in range(3)])
                    for m in range(3):
                        for n in range(3):
                            coefs[place, 3 * m + n] = combine(
                                [TAPS[ii][m] for ii in range(3)], [partial[ii][n] for ii in range(3)]) * (1.0 / 9.0)

                total = placed[row, pl.ds(pl.multiple_of(BLOCK * tile, BLOCK), BLOCK), :]
                for m in range(3):
                    for n in range(3):
                        total = total + coefs[place, 3 * m + n] * wide_parent[row + m, pl.ds(7 + BLOCK * tile + n, BLOCK, stride=1), :]
                covered = (cols >= 0) & (cols < FOOT_Y) & (cols * 0 + k >= 0) & (cols * 0 + k < FOOT_X)
                own = parent[row, pl.ds(pl.multiple_of(BLOCK * tile, BLOCK), BLOCK), :]
                parent_new[row, pl.ds(pl.multiple_of(BLOCK * tile, BLOCK), BLOCK), :] = jnp.where(
                    covered, own + weight * (total - own), own)

            def fix_rows(first, count):
                @pl.loop(jnp.maximum(first, 0), jnp.minimum(first + count, TILE))
                def _(row):
                    for tile in range(3):
                        fix(row, tile, 3 * row + tile)

            def fix_cols(first, count):
                low = lax.div(jnp.maximum(first, 0), BLOCK)
                high = lax.div(jnp.minimum(first + count, TILE) - 1, BLOCK) + 1

                @pl.loop(low, high)
                def _(tile):
                    @pl.loop(0, TILE)
                    def _(row):
                        fix(row, tile, 3 * row + tile)

            for touches, fixer, first, count in (
                (near_row, fix_rows, -first_k, 1), (far_row, fix_rows, FOOT_X - move_x - first_k, move_x),
                (near_col, fix_cols, -first_l, 1), (far_col, fix_cols, FOOT_Y - move_y - first_l, move_y),
            ):
                @pl.when(touches)
                def _():
                    fixer(first, count)


def blocked(*dims):
    zeros = (0,) * len(dims)
    return pl.BlockSpec((*dims, LANES), lambda chunk: (*zeros, chunk))


def local(parent_field, nest_field, anchor, displacement, feedback_weight, rim_weight):
    f32 = jnp.float32
    smem = pl.BlockSpec(memory_space=pltpu.SMEM)
    tile = blocked(TILE, TILE)
    prepared = ((BLOCK, BLOCK), (5, 4, 16), (5, 10, 8))
    average, send_x, send_y = pl.pallas_call(
        prepare_kernel,
        grid=(CHUNKS,),
        out_shape=tuple(jax.ShapeDtypeStruct((*dims, CHAN), f32) for dims in prepared),
        in_specs=[smem, smem, smem, tile, tile],
        out_specs=tuple(blocked(*dims) for dims in prepared),
        scratch_shapes=[pltpu.VMEM((TILE, TILE + 2 * PAD, LANES), f32)],
        name="prepare",
    )(anchor, displacement, rim_weight, nest_field, parent_field)
    order = jnp.where(anchor[0] == TOP, anchor[1] // BLOCK, TILES_Y + anchor[0] // BLOCK)
    crossed = lax.switch(order, [variant(v) for v in VARIANTS], nest_field, parent_field, average, send_x, send_y)
    shape = jax.ShapeDtypeStruct((TILE, TILE, CHAN), f32)
    return pl.pallas_call(
        finish_kernel,
        grid=(CHUNKS,),
        out_shape=(shape, shape),
        in_specs=[smem, smem, smem, tile, tile, blocked(1), *(blocked(*dims) for dims in CROSSED)],
        out_specs=(tile, tile),
        scratch_shapes=[
            pltpu.VMEM((TILE + MARGIN, TILE + 8, LANES), f32),
            pltpu.VMEM((TILE + 2, TILE + 16, LANES), f32),
            pltpu.VMEM((TILE, TILE, LANES), f32),
            pltpu.VMEM((3 * TILE, 9, BLOCK, LANES), f32),
            pltpu.VMEM((16, LANES), f32),
            pltpu.VMEM((4, TILE, LANES), f32),
            pltpu.VMEM((10, 8, LANES), f32),
            pltpu.VMEM((10, 8, LANES), f32),
        ],
        name="finish",
    )(anchor, displacement, rim_weight, parent_field, nest_field, feedback_weight.reshape(1, CHAN), *crossed)


VARIANTS = tuple(range(32))
TILES_Y = 16


def solution(mesh):
    in_specs = (P("px", "py", None), P("px", "py", None), P(), P(), P(), P())
    out_specs = (P("px", "py", None), P("px", "py", None))
    return jax.shard_map(local, mesh=mesh, in_specs=in_specs, out_specs=out_specs, check_vma=False)
```

```python
import functools

import jax
import jax.numpy as jnp
from jax import lax
from jax.experimental import pallas as pl
from jax.experimental.pallas import tpu as pltpu
from jax.sharding import PartitionSpec as P

REFINE = 3
TILE = 24
BLOCK = 8
LANES = 128
CHUNKS = 5
CHAN = CHUNKS * LANES
RIM_CELLS = 3
MARGIN = 2 * REFINE
NX, NY = 8, 16
FOOT_X, FOOT_Y = NX * BLOCK, NY * BLOCK
FINE_X, FINE_Y = NX * TILE, NY * TILE
PAD = 16
WINDOW_ORDER = ((0, 0), (0, 1), (0, 2), (1, 1), (1, 2))
TOP = 125
MESH = pl.DeviceIdType.MESH
TAPS = ((1 / 3, 2 / 3, 0.0), (0.0, 1.0, 0.0), (0.0, 2 / 3, 1 / 3))


def combine(taps, values):
    total = None
    for tap, value in zip(taps, values):
        if tap == 0.0:
            continue
        term = value if tap == 1.0 else tap * value
        total = term if total is None else total + term
    return total


class Dim:
    def __init__(self, count, q, low, high):
        self.count, self.q, self.low, self.high = count, q, low, high
        self.fixed = low == high
        self.second_from = 2 if BLOCK + high + 1 + 9 < TILE else 1
        first, last = BLOCK * q + low, BLOCK * q + high + 1
        self.near = sorted({first // TILE, (last + 2) // TILE})
        far = BLOCK * (count - 1) + 6
        self.far = sorted({(first + far) // TILE, (last + far + 3) // TILE})

    def split(self, index):
        g = index + self.q
        return lax.div(g, 3), lax.rem(g, 3)

    def used(self, index):
        return (3 * index + 2 >= self.q) & (3 * index - 1 - self.q < self.count)

    def strip_role(self, index):
        near, either, place = jnp.bool_(False), jnp.bool_(False), jnp.int32(0)
        for owners in (self.near, self.far):
            for order, owner in enumerate(owners):
                hit = index == owner
                either = either | hit
                if owners is self.near:
                    near = near | hit
                if order:
                    place = jnp.where(hit, order, place)
        return near, either, place


class Family:
    def __init__(self, sends, send, receives, receive, maybe_self=False):
        self.sends, self.send, self.receives, self.receive, self.maybe_self = sends, send, receives, receive, maybe_self


def each(count, body):
    if count == 1:
        body(jnp.int32(0))
    elif count:
        pl.loop(0, count)(body)


def send_kernel(
    dim_x, dim_y,
    anchor_ref, nest, parent_edges, parent_corners, average, send_x, send_y,
    arrived, nest_below, nest_beside, nest_corner, edges, corners, recv_x, recv_y,
    relay, compact,
    first_send, first_recv, next_send, next_recv, nest_send, nest_recv, edge_send, edge_recv, wx_send, wx_recv, wy_send, wy_recv,
):
    me_x, me_y = lax.axis_index("px"), lax.axis_index("py")

    def averages(dim, index, at, source, target, active, send_sem, recv_sem):
        owner, phase = dim.split(index)

        def source_of(slot):
            return 3 * index - 1 + slot - dim.q

        def valid(slot):
            return (source_of(slot) >= 0) & (source_of(slot) < dim.count) & dim.used(index)

        if not dim.fixed:
            return [Family(
                2, lambda i: (
                    active & ((i == 0) | (phase == 2)), at(owner + i), source(0, BLOCK),
                    target((phase + 1) * (1 - i), 0, BLOCK), send_sem.at[i], recv_sem.at[(phase + 1) * (1 - i)]),
                4, lambda i: (valid(i), at(source_of(i)), target(i, 0, BLOCK), recv_sem.at[i]), True)]
        cut = BLOCK - dim.low
        return [
            Family(
                1, lambda i: (
                    active & (phase < 2), at(owner), source(0, BLOCK), target(phase + 1, 0, BLOCK),
                    send_sem.at[0], recv_sem.at[phase + 1]),
                2, lambda i: (valid(i + 1), at(source_of(i + 1)), target(i + 1, 0, BLOCK), recv_sem.at[i + 1]), True),
            Family(
                1, lambda i: (
                    active & (phase == 2), at(owner), source(0, cut), target(3, 0, cut), send_sem.at[0], recv_sem.at[3]),
                1, lambda i: (valid(3), at(source_of(3)), target(3, 0, cut), recv_sem.at[3]), True),
            Family(
                1, lambda i: (
                    active & (phase == 2), at(owner + 1), source(cut, BLOCK - cut), target(0, cut, BLOCK - cut),
                    send_sem.at[1], recv_sem.at[0]),
                1, lambda i: (valid(0), at(source_of(0)), target(0, cut, BLOCK - cut), recv_sem.at[0]), True),
        ]

    always = me_x >= 0
    first = averages(
        dim_y, me_y, lambda y: (me_x, y), lambda start, size: average.at[:, pl.ds(start, size), :],
        lambda slot, start, size: relay.at[slot, :, pl.ds(start, size), :], always, first_send, first_recv)
    following = averages(
        dim_x, me_x, lambda x: (x, me_y), lambda start, size: compact.at[pl.ds(start, size)],
        lambda slot, start, size: arrived.at[slot, pl.ds(start, size)], dim_y.used(me_y), next_send, next_recv)
    for family in following:
        inner = family.receive
        family.receive = lambda i, inner=inner: (inner(i)[0] & dim_y.used(me_y), *inner(i)[1:])

    def inside(x, y):
        return (x >= 0) & (x < NX) & (y >= 0) & (y < NY)

    def shift(count, step, source, target, send_sem, recv_sem):
        def send(i):
            x, y = me_x + step(i)[0], me_y + step(i)[1]
            return inside(x, y), (x, y), source(i), target(i), send_sem(i), recv_sem(i)

        def receive(i):
            x, y = me_x - step(i)[0], me_y - step(i)[1]
            return inside(x, y), (x, y), target(i), recv_sem(i)

        return Family(count, send, count, receive)

    halos = []
    for order, (step_x, step_y) in enumerate(((1, 0), (0, 1), (1, 1))):
        rows, cols = (MARGIN if step_x else TILE), (MARGIN if step_y else TILE)
        lands = (nest_below, nest_beside, nest_corner)[order].at[:, pl.ds(0, cols), :]
        halos.append(shift(
            1, lambda i, step_x=step_x, step_y=step_y: (-step_x, -step_y),
            lambda i, rows=rows, cols=cols: nest.at[pl.ds(0, rows), pl.ds(0, cols), :], lambda i, lands=lands: lands,
            lambda i, order=order: nest_send.at[order], lambda i, order=order: nest_recv.at[order]))
    halos.append(shift(
        4, lambda i: ((1 - lax.div(i, 2)) * (2 * i - 1), lax.div(i, 2) * (2 * i - 5)),
        lambda i: parent_edges.at[i], lambda i: edges.at[i], lambda i: edge_send.at[i], lambda i: edge_recv.at[i]))
    halos.append(shift(
        4, lambda i: (2 * lax.div(i, 2) - 1, 2 * lax.rem(i, 2) - 1),
        lambda i: parent_corners.at[i], lambda i: corners.at[i], lambda i: edge_send.at[4 + i], lambda i: edge_recv.at[4 + i]))

    def windows(dim, index, along, along_index, swap, source, target, send_sem, recv_sem):
        near, strip, place = dim.strip_role(index)
        device = (lambda a, b: (b, a)) if swap else (lambda a, b: (a, b))
        places = max(len(dim.near), len(dim.far))
        owner, phase = along.split(along_index)

        def send(i):
            second = lax.div(i, 3)
            aim = lax.rem(i, 3) + second
            to = 3 * (along_index - second) + aim - along.q
            has = strip & (to >= 0) & (to < along.count)
            if along.second_from == 2:
                has = has & (i != 3)
            return has, device(jnp.where(near, 0, dim.count - 1), to), source.at[i], target.at[place, second], send_sem.at[i], recv_sem.at[place, second]

        def receive(i):
            at, second = lax.div(i, 2), lax.rem(i, 2)
            across = jnp.int32(-1)
            for order in range(places):
                here_near = dim.near[order] if order < len(dim.near) else -1
                here_far = dim.far[order] if order < len(dim.far) else -1
                across = jnp.where(at == order, jnp.where(index == 0, here_near, here_far), across)
            has = ((index == 0) | (index == dim.count - 1)) & (across >= 0)
            has = has & ((second == 0) | ((phase >= along.second_from) & (owner + 1 < along.count)))
            return has, device(across, owner + second), target.at[at, second], recv_sem.at[at, second]

        return Family(5, send, 2 * places, receive, True)

    rims = [
        windows(dim_x, me_x, dim_y, me_y, False, send_x, recv_x, wx_send, wx_recv),
        windows(dim_y, me_y, dim_x, me_x, True, send_y, recv_y, wy_send, wy_recv),
    ]
    families = first + rims + following + halos

    def is_me(device):
        return (device[0] == me_x) & (device[1] == me_y)

    barrier = pltpu.get_barrier_semaphore()
    for family in families:
        def tell(i):
            has, device, _, _ = family.receive(i)

            @pl.when(has & jnp.logical_not(is_me(device)))
            def _():
                pl.semaphore_signal(barrier, inc=1, device_id=device, device_id_type=MESH)

        each(family.receives, tell)

    expected = jnp.int32(0)
    for family in families:
        def expect(i, count):
            has, device, *_ = family.send(i)
            return count + jnp.where(has & jnp.logical_not(is_me(device)), 1, 0)

        if family.sends == 1:
            expected = expect(jnp.int32(0), expected)
        else:
            expected = lax.fori_loop(0, family.sends, expect, expected)
    pl.semaphore_wait(barrier, expected)

    def remote(entry):
        _, device, src, dst, send_sem, recv_sem = entry
        return pltpu.make_async_remote_copy(
            src_ref=src, dst_ref=dst, send_sem=send_sem, recv_sem=recv_sem, device_id=device, device_id_type=MESH)

    def start(family):
        def body(i):
            entry = family.send(i)
            own = is_me(entry[1])

            @pl.when(entry[0] & jnp.logical_not(own))
            def _():
                remote(entry).start()

            if family.maybe_self:
                @pl.when(entry[0] & own)
                def _():
                    pltpu.make_async_copy(entry[2], entry[3], entry[5]).start()

        each(family.sends, body)

    def finish(family):
        def body(i):
            has, _, dst, recv_sem = family.receive(i)

            @pl.when(has)
            def _():
                pltpu.make_async_copy(dst, dst, recv_sem).wait()

        each(family.receives, body)

    def drain(family):
        def body(i):
            entry = family.send(i)

            @pl.when(entry[0] & jnp.logical_not(is_me(entry[1])))
            def _():
                remote(entry).wait_send()

        each(family.sends, body)

    for family in first + rims:
        start(family)
    for family in first:
        finish(family)

    @pl.when(dim_y.used(me_y))
    def _():
        phase_y = anchor_ref[1] - BLOCK * dim_y.q

        @pl.loop(0, BLOCK)
        def _(row):
            whole = jnp.concatenate([relay[slot, row] for slot in range(4)], axis=0)
            compact[row] = pltpu.roll(whole, 3 * BLOCK + phase_y, 0)[:TILE]

    for family in following + halos:
        start(family)
    for family in rims + halos + following:
        finish(family)
    for family in families:
        drain(family)


CROSSED = (
    (4, BLOCK, TILE), (MARGIN, TILE), (TILE, 8), (MARGIN, 8), (4, TILE), (4, 8), (2, 2, 4, 16), (2, 2, 10, 8),
)


def free(count, q):
    return Dim(count, q, max(0, 1 - BLOCK * q), min(BLOCK - 1, TOP - 1 - BLOCK * q))


def variant(order):
    if order < 16:
        dims = Dim(NX, TOP // BLOCK, TOP % BLOCK, TOP % BLOCK), free(NY, order)
    else:
        dims = free(NX, order - 16), Dim(NY, TOP // BLOCK, TOP % BLOCK, TOP % BLOCK)
    dma = pltpu.SemaphoreType.DMA
    hbm = pl.BlockSpec(memory_space=pl.ANY)
    return pl.pallas_call(
        functools.partial(send_kernel, *dims),
        name=f"send_{order}",
        out_shape=tuple(jax.ShapeDtypeStruct((*dims, CHAN), jnp.float32) for dims in CROSSED),
        in_specs=[pl.BlockSpec(memory_space=pltpu.SMEM)] + [hbm] * 6,
        out_specs=(hbm,) * len(CROSSED),
        scratch_shapes=[
            pltpu.VMEM((4, BLOCK, BLOCK, CHAN), jnp.float32), pltpu.VMEM((BLOCK, TILE, CHAN), jnp.float32),
            dma((2,)), dma((4,)), dma((2,)), dma((4,)), dma((3,)), dma((3,)), dma((8,)), dma((8,)),
            dma((5,)), dma((2, 2)), dma((5,)), dma((2, 2)),
        ],
        compiler_params=pltpu.CompilerParams(collective_id=order, has_side_effects=True),
    )


def facts_of(anchor_ref, move_ref):
    move = move_ref[0], move_ref[1]
    anchor = anchor_ref[0], anchor_ref[1]
    corner = anchor[0] + move[0], anchor[1] + move[1]
    q = lax.div(anchor[0], BLOCK), lax.div(anchor[1], BLOCK)
    phase = anchor[0] - BLOCK * q[0], anchor[1] - BLOCK * q[1]
    return move, corner, q, phase


def blender(rim_ref):
    rims = [rim_ref[level] for level in range(RIM_CELLS)]

    def blend_of(distance):
        value = jnp.where(distance == 2, rims[2], 0.0)
        value = jnp.where(distance == 1, rims[1], value)
        return jnp.where(distance == 0, rims[0], value)

    return blend_of


def iota(rows):
    return lax.broadcasted_iota(jnp.int32, (rows, LANES), 0)


def prepare_kernel(anchor_ref, move_ref, rim_ref, nest, parent, average, send_x, send_y, edges, corners, route, padded):
    me_x, me_y = lax.axis_index("px"), lax.axis_index("py")
    (move_x, move_y), (corner_x, corner_y), _, (phase_x, phase_y) = facts_of(anchor_ref, move_ref)
    blend_of = blender(rim_ref)
    order = jnp.where(anchor_ref[0] == TOP, lax.div(anchor_ref[1], BLOCK), 16 + lax.div(anchor_ref[0], BLOCK))
    route[0] = order

    @pl.loop(0, BLOCK, unroll=4)
    def _(k):
        row = REFINE * (BLOCK * me_x + k - move_x)
        col = REFINE * (BLOCK * me_y + iota(BLOCK) - move_y)
        total = None
        for ii in range(3):
            for jj in range(3):
                keep = (1.0 - blend_of(jnp.minimum(col + jj, row + ii))) * (1.0 / 9.0)
                term = keep * nest[REFINE * k + ii, pl.ds(jj, BLOCK, stride=REFINE), :]
                total = term if total is None else total + term
        average[k] = total

    edges[0], edges[1] = parent[0], parent[TILE - 1]
    for row in range(TILE):
        for side in range(2):
            col = side * (TILE - 1)
            edges[2 + side, row:row + 1, :] = parent[row, col:col + 1, :]
    for order in range(4):
        row, col = order // 2 * (TILE - 1), order % 2 * (TILE - 1)
        corners[order, 0:1, :] = parent[row, col:col + 1, :]

    def strip(corner, foot, me):
        first = corner - 1 - TILE * me
        near = (first <= TILE - 1) & (first + 2 >= 0)
        far = (first + foot - 2 <= TILE - 1) & (first + foot + 1 >= 0)
        return near | far, first + jnp.where(near, 0, foot - 2)

    strip_x, first_row = strip(corner_x, FOOT_X, me_x)
    strip_y, first_col = strip(corner_y, FOOT_Y, me_y)

    @pl.when(strip_x | strip_y)
    def _():
        @pl.loop(0, TILE, unroll=8)
        def _(row):
            padded[row, pl.ds(PAD, TILE), :] = parent[row]

    @pl.when(strip_x)
    def _():
        for order, (second, phase) in enumerate(WINDOW_ORDER):
            start = PAD + BLOCK * phase - TILE * second + phase_y + move_y - 1
            for m in range(4):
                send_x[order, m] = padded[jnp.clip(first_row + m, 0, TILE - 1), pl.ds(jnp.clip(start, 0, TILE + PAD), 16, stride=1), :]

    @pl.when(strip_y)
    def _():
        for order, (second, phase) in enumerate(WINDOW_ORDER):
            first = BLOCK * phase - TILE * second + phase_x + move_x - 1
            for m in range(10):
                send_y[order, m] = padded[jnp.clip(first + m, 0, TILE - 1), pl.ds(jnp.clip(PAD + first_col, 0, TILE + PAD), 8, stride=1), :]


def finish_kernel(
    anchor_ref, move_ref, rim_ref,
    parent, nest, feed, arrived, nest_below, nest_beside, nest_corner, edges, corners, recv_x, recv_y,
    parent_new, nest_new,
    wide_nest, wide_parent, placed, coefs, merged_x, fine_x, merged_y, fine_y,
):
    me_x, me_y = lax.axis_index("px"), lax.axis_index("py")
    (move_x, move_y), (corner_x, corner_y), (q_x, q_y), (phase_x, phase_y) = facts_of(anchor_ref, move_ref)
    blend_of = blender(rim_ref)

    @pl.loop(0, TILE, unroll=8)
    def _(row):
        wide_nest[row, pl.ds(0, TILE), :] = nest[row]
        wide_nest[row, pl.ds(TILE, 8), :] = nest_beside[row]

    @pl.loop(0, MARGIN, unroll=6)
    def _(row):
        wide_nest[TILE + row, pl.ds(0, TILE), :] = nest_below[row]
        wide_nest[TILE + row, pl.ds(TILE, 8), :] = nest_corner[row]

    @pl.loop(0, TILE, unroll=8)
    def _(row):
        nest_new[row] = wide_nest[row + REFINE * move_x, pl.ds(REFINE * move_y, TILE, stride=1), :]

    def blended(row, cols, shifted, interp):
        entered = (cols >= FINE_Y - REFINE * move_y) | (cols * 0 + row >= FINE_X - REFINE * move_x)
        moved = jnp.where(entered, interp, shifted)
        distance = jnp.minimum(jnp.minimum(cols, FINE_Y - 1 - cols), jnp.minimum(row, FINE_X - 1 - row))
        return moved + blend_of(distance) * (interp - moved)

    def edge_columns(at_near):
        rel_row = BLOCK * lax.rem(me_x + q_x, 3) + phase_x + move_x - 1
        columns = iota(BLOCK)
        if at_near:
            first_col, step, bound, base = 0, columns, TILE * (lax.div(q_y, 3) + 1), corner_y - 1
        else:
            first_col, step = TILE - BLOCK, columns - 2
            bound, base = TILE * (lax.div(q_y + NY - 1, 3) + 1), corner_y - 1 + FOOT_Y - 2
        beyond = base + columns >= bound
        cell = jnp.where(step >= 3, 1, 0)
        sub = step - 3 * cell
        taps = []
        for n in range(3 if at_near else 4):
            m = n - cell
            left = jnp.where(m == 0, 1 / 3, jnp.where(m == 1, 2 / 3, 0.0))
            mid = jnp.where(m == 1, 1.0, 0.0)
            right = jnp.where(m == 1, 2 / 3, jnp.where(m == 2, 1 / 3, 0.0))
            taps.append(jnp.where(sub == 0, left, jnp.where(sub == 1, mid, right)))
        in_strip = (step >= 0) & (step < (3 if at_near else 6))
        for m in range(10):
            second = jnp.where(rel_row + m >= TILE, 1, 0)
            merged_y[m] = jnp.where(beyond, recv_y[1, second, m], recv_y[0, second, m])
            total = None
            for n, tap in enumerate(taps):
                term = tap * jnp.broadcast_to(merged_y[m, n:n + 1, :], (BLOCK, LANES))
                total = term if total is None else total + term
            fine_y[m] = total

        @pl.loop(0, BLOCK, unroll=4)
        def _(k):
            for ii in range(3):
                row = REFINE * k + ii
                interp = combine(TAPS[ii], [fine_y[k + m] for m in range(3)])
                shifted = wide_nest[row + REFINE * move_x, pl.ds(first_col + REFINE * move_y, BLOCK, stride=1), :]
                value = blended(TILE * me_x + row, TILE * me_y + first_col + columns, shifted, interp)
                nest_new[row, pl.ds(first_col, BLOCK), :] = jnp.where(in_strip, value, shifted)

    def edge_rows(at_near):
        rel_col = BLOCK * lax.rem(me_y + q_y, 3) + phase_y + move_y - 1
        second = rel_col + iota(16) >= TILE
        cols = TILE * me_y + iota(TILE)
        if at_near:
            bound, first_row, cells = TILE * (lax.div(q_x, 3) + 1), corner_x - 1, 1
        else:
            bound, first_row, cells = TILE * (lax.div(q_x + NX - 1, 3) + 1), corner_x - 1 + FOOT_X - 2, 2
        for m in range(cells + 2):
            place = jnp.where(first_row + m >= bound, 1, 0)
            merged_x[...] = jnp.where(second, recv_x[place, 1, m], recv_x[place, 0, m])
            for jj in range(3):
                fine_x[m, pl.ds(jj, BLOCK, stride=REFINE), :] = combine(
                    TAPS[jj], [merged_x[pl.ds(n, BLOCK), :] for n in range(3)])
        for k in range(cells):
            for ii in range(3):
                row = (0 if at_near else TILE - 3 * cells) + 3 * k + ii
                interp = combine(TAPS[ii], [fine_x[k + m] for m in range(3)])
                shifted = wide_nest[row + REFINE * move_x, pl.ds(REFINE * move_y, TILE, stride=1), :]
                nest_new[row] = blended(TILE * me_x + row, cols, shifted, interp)

    for at_near in (True, False):
        @pl.when(me_y == (0 if at_near else NY - 1))
        def _():
            edge_columns(at_near)
    for at_near in (True, False):
        @pl.when(me_x == (0 if at_near else NX - 1))
        def _():
            edge_rows(at_near)

    first_k, first_l = TILE * me_x - corner_x, TILE * me_y - corner_y
    touched = (first_k < FOOT_X) & (first_k + TILE > 0) & (first_l < FOOT_Y) & (first_l + TILE > 0)

    @pl.when(jnp.logical_not(touched))
    def _():
        parent_new[...] = parent[...]

    @pl.when(touched)
    def _():
        l = first_l + iota(TILE)
        weight = feed[...]

        @pl.loop(0, TILE, unroll=8)
        def _(row):
            k = l * 0 + (first_k + row)
            covered = (l >= 0) & (l < FOOT_Y) & (k >= 0) & (k < FOOT_X)
            usable = covered & (l < FOOT_Y - move_y) & (k < FOOT_X - move_x)
            at = row + BLOCK - phase_x
            slot_x, in_x = lax.div(at, BLOCK), lax.rem(at, BLOCK)
            whole = jnp.where(usable, arrived[slot_x, in_x], 0.0)
            own = parent[row]
            placed[row] = whole
            parent_new[row] = jnp.where(covered, own + weight * (whole - own), own)

        near_row = (first_k <= 0) & (first_k + TILE > 0)
        near_col = (first_l <= 0) & (first_l + TILE > 0)
        far_row = (first_k < FOOT_X) & (first_k + TILE > FOOT_X - move_x)
        far_col = (first_l < FOOT_Y) & (first_l + TILE > FOOT_Y - move_y)

        @pl.when(near_row | near_col | far_row | far_col)
        def _():
            for row in range(TILE):
                wide_parent[row + 1, pl.ds(8, TILE), :] = parent[row]
                wide_parent[row + 1, pl.ds(7, 1), :] = edges[3, row:row + 1, :]
                wide_parent[row + 1, pl.ds(8 + TILE, 1), :] = edges[2, row:row + 1, :]
            for down, row in ((1, 0), (0, TILE + 1)):
                wide_parent[row, pl.ds(8, TILE), :] = edges[down]
                wide_parent[row, pl.ds(7, 1), :] = corners[2 * down + 1, 0:1, :]
                wide_parent[row, pl.ds(8 + TILE, 1), :] = corners[2 * down, 0:1, :]

            def weigh(row, tile, place):
                cols = first_l + BLOCK * tile + iota(BLOCK)
                k = first_k + row
                entered = (cols >= FOOT_Y - move_y) | (cols * 0 + k >= FOOT_X - move_x)
                partial = []
                for ii in range(3):
                    weights = [
                        jnp.where(entered, 1.0, blend_of(jnp.minimum(REFINE * cols + jj, REFINE * k + ii)))
                        for jj in range(3)
                    ]
                    partial.append([combine([TAPS[jj][n] for jj in range(3)], weights) for n in range(3)])
                for m in range(3):
                    for n in range(3):
                        coefs[place, 3 * m + n] = combine(
                            [TAPS[ii][m] for ii in range(3)], [partial[ii][n] for ii in range(3)]) * (1.0 / 9.0)

            def fix(row, tile, place):
                cols = first_l + BLOCK * tile + iota(BLOCK)
                k = first_k + row
                total = placed[row, pl.ds(pl.multiple_of(BLOCK * tile, BLOCK), BLOCK), :]
                for m in range(3):
                    for n in range(3):
                        total = total + coefs[place, 3 * m + n] * wide_parent[row + m, pl.ds(7 + BLOCK * tile + n, BLOCK, stride=1), :]
                covered = (cols >= 0) & (cols < FOOT_Y) & (cols * 0 + k >= 0) & (cols * 0 + k < FOOT_X)
                own = parent[row, pl.ds(pl.multiple_of(BLOCK * tile, BLOCK), BLOCK), :]
                parent_new[row, pl.ds(pl.multiple_of(BLOCK * tile, BLOCK), BLOCK), :] = jnp.where(
                    covered, own + weight * (total - own), own)

            def fix_rows(first, count, work):
                @pl.loop(jnp.maximum(first, 0), jnp.minimum(first + count, TILE))
                def _(row):
                    for tile in range(3):
                        work(row, tile, 3 * row + tile)

            def fix_cols(first, count, work):
                low = lax.div(jnp.maximum(first, 0), BLOCK)
                high = lax.div(jnp.minimum(first + count, TILE) - 1, BLOCK) + 1

                @pl.loop(low, high)
                def _(tile):
                    @pl.loop(0, TILE, unroll=4)
                    def _(row):
                        work(row, tile, 3 * row + tile)

            for touches, fixer, first, count in (
                (near_row, fix_rows, -first_k, 1), (far_row, fix_rows, FOOT_X - move_x - first_k, move_x),
                (near_col, fix_cols, -first_l, 1), (far_col, fix_cols, FOOT_Y - move_y - first_l, move_y),
            ):
                @pl.when(touches & (pl.program_id(0) == 0))
                def _():
                    fixer(first, count, weigh)

                @pl.when(touches)
                def _():
                    fixer(first, count, fix)


def blocked(*dims):
    zeros = (0,) * len(dims)
    return pl.BlockSpec((*dims, LANES), lambda chunk: (*zeros, chunk))


def local(parent_field, nest_field, anchor, displacement, feedback_weight, rim_weight):
    f32 = jnp.float32
    smem = pl.BlockSpec(memory_space=pltpu.SMEM)
    tile = blocked(TILE, TILE)
    prepared = ((BLOCK, BLOCK), (5, 4, 16), (5, 10, 8), (4, TILE), (4, 8))
    average, send_x, send_y, parent_edges, parent_corners, route = pl.pallas_call(
        prepare_kernel,
        grid=(CHUNKS,),
        out_shape=(
            *(jax.ShapeDtypeStruct((*dims, CHAN), f32) for dims in prepared), jax.ShapeDtypeStruct((1,), jnp.int32)),
        in_specs=[smem, smem, smem, tile, tile],
        out_specs=(*(blocked(*dims) for dims in prepared), smem),
        scratch_shapes=[pltpu.VMEM((TILE, TILE + 2 * PAD, LANES), f32)],
        name="prepare",
    )(anchor, displacement, rim_weight, nest_field, parent_field)
    crossed = lax.switch(
        route[0], [variant(v) for v in VARIANTS], anchor, nest_field, parent_edges, parent_corners, average, send_x, send_y)
    shape = jax.ShapeDtypeStruct((TILE, TILE, CHAN), f32)
    return pl.pallas_call(
        finish_kernel,
        grid=(CHUNKS,),
        out_shape=(shape, shape),
        in_specs=[smem, smem, smem, tile, tile, blocked(1), *(blocked(*dims) for dims in CROSSED)],
        out_specs=(tile, tile),
        scratch_shapes=[
            pltpu.VMEM((TILE + MARGIN, TILE + 8, LANES), f32),
            pltpu.VMEM((TILE + 2, TILE + 16, LANES), f32),
            pltpu.VMEM((TILE, TILE, LANES), f32),
            pltpu.VMEM((3 * TILE, 9, BLOCK, LANES), f32),
            pltpu.VMEM((16, LANES), f32),
            pltpu.VMEM((4, TILE, LANES), f32),
            pltpu.VMEM((10, 8, LANES), f32),
            pltpu.VMEM((10, 8, LANES), f32),
        ],
        name="finish",
    )(anchor, displacement, rim_weight, parent_field, nest_field, feedback_weight.reshape(1, CHAN), *crossed)


VARIANTS = tuple(range(32))


def solution(mesh):
    in_specs = (P("px", "py", None), P("px", "py", None), P(), P(), P(), P())
    out_specs = (P("px", "py", None), P("px", "py", None))
    return jax.shard_map(local, mesh=mesh, in_specs=in_specs, out_specs=out_specs, check_vma=False)
```

```python
import functools

import jax
import jax.numpy as jnp
from jax import lax
from jax.experimental import pallas as pl
from jax.experimental.pallas import tpu as pltpu
from jax.sharding import PartitionSpec as P

REFINE = 3
TILE = 24
BLOCK = 8
LANES = 128
CHUNKS = 5
CHAN = CHUNKS * LANES
RIM_CELLS = 3
MARGIN = 2 * REFINE
NX, NY = 8, 16
FOOT_X, FOOT_Y = NX * BLOCK, NY * BLOCK
FINE_X, FINE_Y = NX * TILE, NY * TILE
PAD = 16
WINDOW_ORDER = ((0, 0), (0, 1), (0, 2), (1, 1), (1, 2))
TOP = 125
MESH = pl.DeviceIdType.MESH
TAPS = ((1 / 3, 2 / 3, 0.0), (0.0, 1.0, 0.0), (0.0, 2 / 3, 1 / 3))


def combine(taps, values):
    total = None
    for tap, value in zip(taps, values):
        if tap == 0.0:
            continue
        term = value if tap == 1.0 else tap * value
        total = term if total is None else total + term
    return total


class Dim:
    def __init__(self, count, q, low, high):
        self.count, self.q, self.low, self.high = count, q, low, high
        self.fixed = low == high
        self.second_from = 2 if BLOCK + high + 1 + 9 < TILE else 1
        first, last = BLOCK * q + low, BLOCK * q + high + 1
        self.near = sorted({first // TILE, (last + 2) // TILE})
        far = BLOCK * (count - 1) + 6
        self.far = sorted({(first + far) // TILE, (last + far + 3) // TILE})

    def split(self, index):
        g = index + self.q
        return lax.div(g, 3), lax.rem(g, 3)

    def used(self, index):
        return (3 * index + 2 >= self.q) & (3 * index - 1 - self.q < self.count)

    def strip_role(self, index):
        near, either, place = jnp.bool_(False), jnp.bool_(False), jnp.int32(0)
        for owners in (self.near, self.far):
            for order, owner in enumerate(owners):
                hit = index == owner
                either = either | hit
                if owners is self.near:
                    near = near | hit
                if order:
                    place = jnp.where(hit, order, place)
        return near, either, place


class Family:
    def __init__(self, sends, send, receives, receive, maybe_self=False):
        self.sends, self.send, self.receives, self.receive, self.maybe_self = sends, send, receives, receive, maybe_self


def each(count, body):
    if count == 1:
        body(jnp.int32(0))
    elif count:
        pl.loop(0, count)(body)


def send_kernel(
    dim_x, dim_y,
    anchor_ref, nest, parent_edges, parent_corners, average, send_x, send_y,
    arrived, nest_below, nest_beside, nest_corner, edges, corners, recv_x, recv_y,
    relay, compact,
    first_send, first_recv, next_send, next_recv, nest_send, nest_recv, edge_send, edge_recv, wx_send, wx_recv, wy_send, wy_recv,
):
    me_x, me_y = lax.axis_index("px"), lax.axis_index("py")

    def averages(dim, index, at, source, target, active, send_sem, recv_sem):
        owner, phase = dim.split(index)

        def source_of(slot):
            return 3 * index - 1 + slot - dim.q

        def valid(slot):
            return (source_of(slot) >= 0) & (source_of(slot) < dim.count) & dim.used(index)

        if not dim.fixed:
            return [Family(
                2, lambda i: (
                    active & ((i == 0) | (phase == 2)), at(owner + i), source(0, BLOCK),
                    target((phase + 1) * (1 - i), 0, BLOCK), send_sem.at[i], recv_sem.at[(phase + 1) * (1 - i)]),
                4, lambda i: (valid(i), at(source_of(i)), target(i, 0, BLOCK), recv_sem.at[i]), True)]
        cut = BLOCK - dim.low
        return [
            Family(
                1, lambda i: (
                    active & (phase < 2), at(owner), source(0, BLOCK), target(phase + 1, 0, BLOCK),
                    send_sem.at[0], recv_sem.at[phase + 1]),
                2, lambda i: (valid(i + 1), at(source_of(i + 1)), target(i + 1, 0, BLOCK), recv_sem.at[i + 1]), True),
            Family(
                1, lambda i: (
                    active & (phase == 2), at(owner), source(0, cut), target(3, 0, cut), send_sem.at[0], recv_sem.at[3]),
                1, lambda i: (valid(3), at(source_of(3)), target(3, 0, cut), recv_sem.at[3]), True),
            Family(
                1, lambda i: (
                    active & (phase == 2), at(owner + 1), source(cut, BLOCK - cut), target(0, cut, BLOCK - cut),
                    send_sem.at[1], recv_sem.at[0]),
                1, lambda i: (valid(0), at(source_of(0)), target(0, cut, BLOCK - cut), recv_sem.at[0]), True),
        ]

    always = me_x >= 0
    first = averages(
        dim_y, me_y, lambda y: (me_x, y), lambda start, size: average.at[:, pl.ds(start, size), :],
        lambda slot, start, size: relay.at[slot, :, pl.ds(start, size), :], always, first_send, first_recv)
    following = averages(
        dim_x, me_x, lambda x: (x, me_y), lambda start, size: compact.at[pl.ds(start, size)],
        lambda slot, start, size: arrived.at[slot, pl.ds(start, size)], dim_y.used(me_y), next_send, next_recv)
    for family in following:
        inner = family.receive
        family.receive = lambda i, inner=inner: (inner(i)[0] & dim_y.used(me_y), *inner(i)[1:])

    def inside(x, y):
        return (x >= 0) & (x < NX) & (y >= 0) & (y < NY)

    def shift(count, step, source, target, send_sem, recv_sem):
        def send(i):
            x, y = me_x + step(i)[0], me_y + step(i)[1]
            return inside(x, y), (x, y), source(i), target(i), send_sem(i), recv_sem(i)

        def receive(i):
            x, y = me_x - step(i)[0], me_y - step(i)[1]
            return inside(x, y), (x, y), target(i), recv_sem(i)

        return Family(count, send, count, receive)

    halos = []
    for order, (step_x, step_y) in enumerate(((1, 0), (0, 1), (1, 1))):
        rows, cols = (MARGIN if step_x else TILE), (MARGIN if step_y else TILE)
        lands = (nest_below, nest_beside, nest_corner)[order].at[:, pl.ds(0, cols), :]
        halos.append(shift(
            1, lambda i, step_x=step_x, step_y=step_y: (-step_x, -step_y),
            lambda i, rows=rows, cols=cols: nest.at[pl.ds(0, rows), pl.ds(0, cols), :], lambda i, lands=lands: lands,
            lambda i, order=order: nest_send.at[order], lambda i, order=order: nest_recv.at[order]))
    halos.append(shift(
        4, lambda i: (jnp.where(i < 2, 2 * i - 1, 0), jnp.where(i < 2, 0, 2 * i - 5)),
        lambda i: parent_edges.at[i], lambda i: edges.at[i], lambda i: edge_send.at[i], lambda i: edge_recv.at[i]))
    halos.append(shift(
        4, lambda i: (jnp.where(i < 2, -1, 1), 2 * i - jnp.where(i < 2, 1, 5)),
        lambda i: parent_corners.at[i], lambda i: corners.at[i], lambda i: edge_send.at[4 + i], lambda i: edge_recv.at[4 + i]))

    def windows(dim, index, along, along_index, swap, source, target, send_sem, recv_sem):
        near, strip, place = dim.strip_role(index)
        device = (lambda a, b: (b, a)) if swap else (lambda a, b: (a, b))
        places = max(len(dim.near), len(dim.far))
        owner, phase = along.split(along_index)

        def send(tail, i):
            second = jnp.where(i >= (2 if tail else 3), 1, 0)
            aim = i - second
            to = 3 * (along_index - second) + aim - along.q
            has = strip & (to >= 0) & (to < along.count)
            if tail and along.second_from == 2:
                has = has & (i != 2)
            return (
                has, device(jnp.where(near, 0, dim.count - 1), to), source(tail, i + second), target(tail, place, second),
                send_sem.at[tail, i], recv_sem.at[tail, place, second])

        def receive(tail, i):
            at = jnp.where(i >= 2, 1, 0)
            second = i - 2 * at
            across = jnp.int32(-1)
            for order in range(places):
                here_near = dim.near[order] if order < len(dim.near) else -1
                here_far = dim.far[order] if order < len(dim.far) else -1
                across = jnp.where(at == order, jnp.where(index == 0, here_near, here_far), across)
            has = ((index == 0) | (index == dim.count - 1)) & (across >= 0)
            if tail:
                has = has & (((second == 0) & (phase < 2)) | ((second == 1) & (phase >= along.second_from)))
            else:
                has = has & ((second == 0) | (phase == 2))
            has = has & (owner + second < along.count)
            return has, device(across, owner + second), target(tail, at, second), recv_sem.at[tail, at, second]

        return [
            Family(4, functools.partial(send, tail), 2 * places, functools.partial(receive, tail), True) for tail in (0, 1)
        ]

    part = (pl.ds(0, 8), pl.ds(8, 2))
    rims = windows(
        dim_x, me_x, dim_y, me_y, False, lambda tail, i: send_x.at[i, :, part[tail], :],
        lambda tail, place, second: recv_x.at[place, second, :, part[tail], :], wx_send, wx_recv)
    rims += windows(
        dim_y, me_y, dim_x, me_x, True, lambda tail, i: send_y.at[i, part[tail], pl.ds(0, 4), :],
        lambda tail, place, second: recv_y.at[place, second, part[tail], pl.ds(0, 4), :], wy_send, wy_recv)
    families = first + rims + following + halos

    def is_me(device):
        return (device[0] == me_x) & (device[1] == me_y)

    barrier = pltpu.get_barrier_semaphore()
    for family in families:
        def tell(i):
            has, device, _, _ = family.receive(i)

            @pl.when(has & jnp.logical_not(is_me(device)))
            def _():
                pl.semaphore_signal(barrier, inc=1, device_id=device, device_id_type=MESH)

        each(family.receives, tell)

    expected = jnp.int32(0)
    for family in families:
        def expect(i, count):
            has, device, *_ = family.send(i)
            return count + jnp.where(has & jnp.logical_not(is_me(device)), 1, 0)

        if family.sends == 1:
            expected = expect(jnp.int32(0), expected)
        else:
            expected = lax.fori_loop(0, family.sends, expect, expected)
    pl.semaphore_wait(barrier, expected)

    def remote(entry):
        _, device, src, dst, send_sem, recv_sem = entry
        return pltpu.make_async_remote_copy(
            src_ref=src, dst_ref=dst, send_sem=send_sem, recv_sem=recv_sem, device_id=device, device_id_type=MESH)

    def start(family):
        def body(i):
            entry = family.send(i)
            own = is_me(entry[1])

            @pl.when(entry[0] & jnp.logical_not(own))
            def _():
                remote(entry).start()

            if family.maybe_self:
                @pl.when(entry[0] & own)
                def _():
                    pltpu.make_async_copy(entry[2], entry[3], entry[5]).start()

        each(family.sends, body)

    def finish(family):
        def body(i):
            has, _, dst, recv_sem = family.receive(i)

            @pl.when(has)
            def _():
                pltpu.make_async_copy(dst, dst, recv_sem).wait()

        each(family.receives, body)

    def drain(family):
        def body(i):
            entry = family.send(i)

            @pl.when(entry[0] & jnp.logical_not(is_me(entry[1])))
            def _():
                remote(entry).wait_send()

        each(family.sends, body)

    for family in first + rims + halos:
        start(family)
    for family in first:
        finish(family)

    @pl.when(dim_y.used(me_y))
    def _():
        phase_y = anchor_ref[1] - BLOCK * dim_y.q

        @pl.loop(0, BLOCK)
        def _(row):
            whole = jnp.concatenate([relay[slot, row] for slot in range(4)], axis=0)
            compact[row] = pltpu.roll(whole, 3 * BLOCK + phase_y, 0)[:TILE]

    for family in following:
        start(family)
    for family in rims + halos + following:
        finish(family)
    for family in families:
        drain(family)


CROSSED = (
    (4, BLOCK, TILE), (MARGIN, TILE), (TILE, 8), (MARGIN, 8), (4, TILE), (4, 8), (2, 2, 4, 16), (2, 2, 10, 8),
)


def free(count, q):
    return Dim(count, q, max(0, 1 - BLOCK * q), min(BLOCK - 1, TOP - 1 - BLOCK * q))


def variant(order):
    if order < 16:
        dims = Dim(NX, TOP // BLOCK, TOP % BLOCK, TOP % BLOCK), free(NY, order)
    else:
        dims = free(NX, order - 16), Dim(NY, TOP // BLOCK, TOP % BLOCK, TOP % BLOCK)
    dma = pltpu.SemaphoreType.DMA
    hbm = pl.BlockSpec(memory_space=pl.ANY)
    return pl.pallas_call(
        functools.partial(send_kernel, *dims),
        name=f"send_{order}",
        out_shape=tuple(jax.ShapeDtypeStruct((*dims, CHAN), jnp.float32) for dims in CROSSED),
        in_specs=[pl.BlockSpec(memory_space=pltpu.SMEM)] + [hbm] * 6,
        out_specs=(hbm,) * len(CROSSED),
        scratch_shapes=[
            pltpu.VMEM((4, BLOCK, BLOCK, CHAN), jnp.float32), pltpu.VMEM((BLOCK, TILE, CHAN), jnp.float32),
            dma((2,)), dma((4,)), dma((2,)), dma((4,)), dma((3,)), dma((3,)), dma((8,)), dma((8,)),
            dma((2, 4)), dma((2, 2, 2)), dma((2, 4)), dma((2, 2, 2)),
        ],
        compiler_params=pltpu.CompilerParams(collective_id=order, has_side_effects=True),
    )


def facts_of(anchor_ref, move_ref):
    move = move_ref[0], move_ref[1]
    anchor = anchor_ref[0], anchor_ref[1]
    corner = anchor[0] + move[0], anchor[1] + move[1]
    q = lax.div(anchor[0], BLOCK), lax.div(anchor[1], BLOCK)
    phase = anchor[0] - BLOCK * q[0], anchor[1] - BLOCK * q[1]
    return move, corner, q, phase


def blender(rim_ref):
    rims = [rim_ref[level] for level in range(RIM_CELLS)]

    def blend_of(distance):
        value = jnp.where(distance == 2, rims[2], 0.0)
        value = jnp.where(distance == 1, rims[1], value)
        return jnp.where(distance == 0, rims[0], value)

    return blend_of


def iota(rows):
    return lax.broadcasted_iota(jnp.int32, (rows, LANES), 0)


def prepare_kernel(anchor_ref, move_ref, rim_ref, nest, parent, average, send_x, send_y, edges, corners, route, padded):
    me_x, me_y = lax.axis_index("px"), lax.axis_index("py")
    (move_x, move_y), (corner_x, corner_y), _, (phase_x, phase_y) = facts_of(anchor_ref, move_ref)
    blend_of = blender(rim_ref)
    order = jnp.where(anchor_ref[0] == TOP, lax.div(anchor_ref[1], BLOCK), 16 + lax.div(anchor_ref[0], BLOCK))
    route[0] = order

    @pl.loop(0, BLOCK, unroll=4)
    def _(k):
        row = REFINE * (BLOCK * me_x + k - move_x)
        col = REFINE * (BLOCK * me_y + iota(BLOCK) - move_y)
        total = None
        for ii in range(3):
            for jj in range(3):
                keep = (1.0 - blend_of(jnp.minimum(col + jj, row + ii))) * (1.0 / 9.0)
                term = keep * nest[REFINE * k + ii, pl.ds(jj, BLOCK, stride=REFINE), :]
                total = term if total is None else total + term
        average[k] = total

    edges[0], edges[1] = parent[0], parent[TILE - 1]
    for row in range(TILE):
        for side in range(2):
            col = side * (TILE - 1)
            edges[2 + side, row:row + 1, :] = parent[row, col:col + 1, :]
    for order in range(4):
        row, col = order // 2 * (TILE - 1), order % 2 * (TILE - 1)
        corners[order, 0:1, :] = parent[row, col:col + 1, :]

    def strip(corner, foot, me):
        first = corner - 1 - TILE * me
        near = (first <= TILE - 1) & (first + 2 >= 0)
        far = (first + foot - 2 <= TILE - 1) & (first + foot + 1 >= 0)
        return near | far, first + jnp.where(near, 0, foot - 2)

    strip_x, first_row = strip(corner_x, FOOT_X, me_x)
    strip_y, first_col = strip(corner_y, FOOT_Y, me_y)

    @pl.when(strip_x | strip_y)
    def _():
        @pl.loop(0, TILE, unroll=8)
        def _(row):
            padded[row, pl.ds(PAD, TILE), :] = parent[row]

    @pl.when(strip_x)
    def _():
        for order, (second, phase) in enumerate(WINDOW_ORDER):
            start = PAD + BLOCK * phase - TILE * second + phase_y + move_y - 1
            for m in range(4):
                send_x[order, m] = padded[jnp.clip(first_row + m, 0, TILE - 1), pl.ds(jnp.clip(start, 0, TILE + PAD), 16, stride=1), :]

    @pl.when(strip_y)
    def _():
        for order, (second, phase) in enumerate(WINDOW_ORDER):
            first = BLOCK * phase - TILE * second + phase_x + move_x - 1
            for m in range(10):
                send_y[order, m] = padded[jnp.clip(first + m, 0, TILE - 1), pl.ds(jnp.clip(PAD + first_col, 0, TILE + PAD), 8, stride=1), :]


def finish_kernel(
    anchor_ref, move_ref, rim_ref,
    parent, nest, feed, arrived, nest_below, nest_beside, nest_corner, edges, corners, recv_x, recv_y,
    parent_new, nest_new,
    wide_nest, wide_parent, placed, coefs, merged_x, fine_x, merged_y, fine_y,
):
    me_x, me_y = lax.axis_index("px"), lax.axis_index("py")
    (move_x, move_y), (corner_x, corner_y), (q_x, q_y), (phase_x, phase_y) = facts_of(anchor_ref, move_ref)
    blend_of = blender(rim_ref)

    @pl.loop(0, TILE, unroll=8)
    def _(row):
        wide_nest[row, pl.ds(0, TILE), :] = nest[row]
        wide_nest[row, pl.ds(TILE, 8), :] = nest_beside[row]

    @pl.loop(0, MARGIN, unroll=6)
    def _(row):
        wide_nest[TILE + row, pl.ds(0, TILE), :] = nest_below[row]
        wide_nest[TILE + row, pl.ds(TILE, 8), :] = nest_corner[row]

    @pl.loop(0, TILE, unroll=8)
    def _(row):
        nest_new[row] = wide_nest[row + REFINE * move_x, pl.ds(REFINE * move_y, TILE, stride=1), :]

    def blended(row, cols, shifted, interp):
        entered = (cols >= FINE_Y - REFINE * move_y) | (cols * 0 + row >= FINE_X - REFINE * move_x)
        moved = jnp.where(entered, interp, shifted)
        distance = jnp.minimum(jnp.minimum(cols, FINE_Y - 1 - cols), jnp.minimum(row, FINE_X - 1 - row))
        return moved + blend_of(distance) * (interp - moved)

    def edge_columns(at_near):
        rel_row = BLOCK * lax.rem(me_x + q_x, 3) + phase_x + move_x - 1
        columns = iota(BLOCK)
        if at_near:
            first_col, step, bound, base = 0, columns, TILE * (lax.div(q_y, 3) + 1), corner_y - 1
        else:
            first_col, step = TILE - BLOCK, columns - 2
            bound, base = TILE * (lax.div(q_y + NY - 1, 3) + 1), corner_y - 1 + FOOT_Y - 2
        beyond = base + columns >= bound
        cell = jnp.where(step >= 3, 1, 0)
        sub = step - 3 * cell
        taps = []
        for n in range(3 if at_near else 4):
            m = n - cell
            left = jnp.where(m == 0, 1 / 3, jnp.where(m == 1, 2 / 3, 0.0))
            mid = jnp.where(m == 1, 1.0, 0.0)
            right = jnp.where(m == 1, 2 / 3, jnp.where(m == 2, 1 / 3, 0.0))
            taps.append(jnp.where(sub == 0, left, jnp.where(sub == 1, mid, right)))
        in_strip = (step >= 0) & (step < (3 if at_near else 6))
        for m in range(10):
            second = jnp.where(rel_row + m >= TILE, 1, 0)
            merged_y[m] = jnp.where(beyond, recv_y[1, second, m], recv_y[0, second, m])
            total = None
            for n, tap in enumerate(taps):
                term = tap * jnp.broadcast_to(merged_y[m, n:n + 1, :], (BLOCK, LANES))
                total = term if total is None else total + term
            fine_y[m] = total

        @pl.loop(0, BLOCK, unroll=4)
        def _(k):
            for ii in range(3):
                row = REFINE * k + ii
                interp = combine(TAPS[ii], [fine_y[k + m] for m in range(3)])
                shifted = wide_nest[row + REFINE * move_x, pl.ds(first_col + REFINE * move_y, BLOCK, stride=1), :]
                value = blended(TILE * me_x + row, TILE * me_y + first_col + columns, shifted, interp)
                nest_new[row, pl.ds(first_col, BLOCK), :] = jnp.where(in_strip, value, shifted)

    def edge_rows(at_near):
        rel_col = BLOCK * lax.rem(me_y + q_y, 3) + phase_y + move_y - 1
        second = rel_col + iota(16) >= TILE
        cols = TILE * me_y + iota(TILE)
        if at_near:
            bound, first_row, cells = TILE * (lax.div(q_x, 3) + 1), corner_x - 1, 1
        else:
            bound, first_row, cells = TILE * (lax.div(q_x + NX - 1, 3) + 1), corner_x - 1 + FOOT_X - 2, 2
        for m in range(cells + 2):
            place = jnp.where(first_row + m >= bound, 1, 0)
            merged_x[...] = jnp.where(second, recv_x[place, 1, m], recv_x[place, 0, m])
            for jj in range(3):
                fine_x[m, pl.ds(jj, BLOCK, stride=REFINE), :] = combine(
                    TAPS[jj], [merged_x[pl.ds(n, BLOCK), :] for n in range(3)])
        for k in range(cells):
            for ii in range(3):
                row = (0 if at_near else TILE - 3 * cells) + 3 * k + ii
                interp = combine(TAPS[ii], [fine_x[k + m] for m in range(3)])
                shifted = wide_nest[row + REFINE * move_x, pl.ds(REFINE * move_y, TILE, stride=1), :]
                nest_new[row] = blended(TILE * me_x + row, cols, shifted, interp)

    for at_near in (True, False):
        @pl.when(me_y == (0 if at_near else NY - 1))
        def _():
            edge_columns(at_near)
    for at_near in (True, False):
        @pl.when(me_x == (0 if at_near else NX - 1))
        def _():
            edge_rows(at_near)

    first_k, first_l = TILE * me_x - corner_x, TILE * me_y - corner_y
    touched = (first_k < FOOT_X) & (first_k + TILE > 0) & (first_l < FOOT_Y) & (first_l + TILE > 0)

    @pl.when(jnp.logical_not(touched))
    def _():
        parent_new[...] = parent[...]

    @pl.when(touched)
    def _():
        l = first_l + iota(TILE)
        weight = feed[...].reshape(1, LANES)

        @pl.loop(0, TILE, unroll=8)
        def _(row):
            k = l * 0 + (first_k + row)
            covered = (l >= 0) & (l < FOOT_Y) & (k >= 0) & (k < FOOT_X)
            usable = covered & (l < FOOT_Y - move_y) & (k < FOOT_X - move_x)
            at = row + BLOCK - phase_x
            slot_x, in_x = lax.div(at, BLOCK), lax.rem(at, BLOCK)
            whole = jnp.where(usable, arrived[slot_x, in_x], 0.0)
            own = parent[row]
            placed[row] = whole
            parent_new[row] = jnp.where(covered, own + weight * (whole - own), own)

        near_row = (first_k <= 0) & (first_k + TILE > 0)
        near_col = (first_l <= 0) & (first_l + TILE > 0)
        far_row = (first_k < FOOT_X) & (first_k + TILE > FOOT_X - move_x)
        far_col = (first_l < FOOT_Y) & (first_l + TILE > FOOT_Y - move_y)

        @pl.when(near_row | near_col | far_row | far_col)
        def _():
            for row in range(TILE):
                wide_parent[row + 1, pl.ds(8, TILE), :] = parent[row]
                wide_parent[row + 1, pl.ds(7, 1), :] = edges[3, row:row + 1, :]
                wide_parent[row + 1, pl.ds(8 + TILE, 1), :] = edges[2, row:row + 1, :]
            for down, row in ((1, 0), (0, TILE + 1)):
                wide_parent[row, pl.ds(8, TILE), :] = edges[down]
                wide_parent[row, pl.ds(7, 1), :] = corners[2 * down + 1, 0:1, :]
                wide_parent[row, pl.ds(8 + TILE, 1), :] = corners[2 * down, 0:1, :]

            def weigh(row, tile, place):
                cols = first_l + BLOCK * tile + iota(BLOCK)
                k = first_k + row
                entered = (cols >= FOOT_Y - move_y) | (cols * 0 + k >= FOOT_X - move_x)
                partial = []
                for ii in range(3):
                    weights = [
                        jnp.where(entered, 1.0, blend_of(jnp.minimum(REFINE * cols + jj, REFINE * k + ii)))
                        for jj in range(3)
                    ]
                    partial.append([combine([TAPS[jj][n] for jj in range(3)], weights) for n in range(3)])
                for m in range(3):
                    for n in range(3):
                        coefs[place, 3 * m + n] = combine(
                            [TAPS[ii][m] for ii in range(3)], [partial[ii][n] for ii in range(3)]) * (1.0 / 9.0)

            def fix(row, tile, place):
                cols = first_l + BLOCK * tile + iota(BLOCK)
                k = first_k + row
                total = placed[row, pl.ds(pl.multiple_of(BLOCK * tile, BLOCK), BLOCK), :]
                for m in range(3):
                    for n in range(3):
                        total = total + coefs[place, 3 * m + n] * wide_parent[row + m, pl.ds(7 + BLOCK * tile + n, BLOCK, stride=1), :]
                covered = (cols >= 0) & (cols < FOOT_Y) & (cols * 0 + k >= 0) & (cols * 0 + k < FOOT_X)
                own = parent[row, pl.ds(pl.multiple_of(BLOCK * tile, BLOCK), BLOCK), :]
                parent_new[row, pl.ds(pl.multiple_of(BLOCK * tile, BLOCK), BLOCK), :] = jnp.where(
                    covered, own + weight * (total - own), own)

            def fix_rows(first, count, work):
                @pl.loop(jnp.maximum(first, 0), jnp.minimum(first + count, TILE))
                def _(row):
                    for tile in range(3):
                        work(row, tile, 3 * row + tile)

            def fix_cols(first, count, work):
                low = lax.div(jnp.maximum(first, 0), BLOCK)
                high = lax.div(jnp.minimum(first + count, TILE) - 1, BLOCK) + 1

                @pl.loop(low, high)
                def _(tile):
                    @pl.loop(0, TILE, unroll=4)
                    def _(row):
                        work(row, tile, 3 * row + tile)

            for touches, fixer, first, count in (
                (near_row, fix_rows, -first_k, 1), (far_row, fix_rows, FOOT_X - move_x - first_k, move_x),
                (near_col, fix_cols, -first_l, 1), (far_col, fix_cols, FOOT_Y - move_y - first_l, move_y),
            ):
                @pl.when(touches & (pl.program_id(0) == 0))
                def _():
                    fixer(first, count, weigh)

                @pl.when(touches)
                def _():
                    fixer(first, count, fix)


def blocked(*dims):
    zeros = (0,) * len(dims)
    return pl.BlockSpec((*dims, LANES), lambda chunk: (*zeros, chunk))


def local(parent_field, nest_field, anchor, displacement, feedback_weight, rim_weight):
    f32 = jnp.float32
    smem = pl.BlockSpec(memory_space=pltpu.SMEM)
    tile = blocked(TILE, TILE)
    prepared = ((BLOCK, BLOCK), (5, 4, 16), (5, 10, 8), (4, TILE), (4, 8))
    average, send_x, send_y, parent_edges, parent_corners, route = pl.pallas_call(
        prepare_kernel,
        grid=(CHUNKS,),
        out_shape=(
            *(jax.ShapeDtypeStruct((*dims, CHAN), f32) for dims in prepared), jax.ShapeDtypeStruct((1,), jnp.int32)),
        in_specs=[smem, smem, smem, tile, tile],
        out_specs=(*(blocked(*dims) for dims in prepared), smem),
        scratch_shapes=[pltpu.VMEM((TILE, TILE + 2 * PAD, LANES), f32)],
        name="prepare",
    )(anchor, displacement, rim_weight, nest_field, parent_field)
    crossed = lax.switch(
        route[0], [variant(v) for v in VARIANTS], anchor, nest_field, parent_edges, parent_corners, average, send_x, send_y)
    shape = jax.ShapeDtypeStruct((TILE, TILE, CHAN), f32)
    return pl.pallas_call(
        finish_kernel,
        grid=(CHUNKS,),
        out_shape=(shape, shape),
        in_specs=[smem, smem, smem, tile, tile, pl.BlockSpec((LANES,), lambda chunk: (chunk,)), *(blocked(*dims) for dims in CROSSED)],
        out_specs=(tile, tile),
        scratch_shapes=[
            pltpu.VMEM((TILE + MARGIN, TILE + 8, LANES), f32),
            pltpu.VMEM((TILE + 2, TILE + 16, LANES), f32),
            pltpu.VMEM((TILE, TILE, LANES), f32),
            pltpu.VMEM((3 * TILE, 9, BLOCK, LANES), f32),
            pltpu.VMEM((16, LANES), f32),
            pltpu.VMEM((4, TILE, LANES), f32),
            pltpu.VMEM((10, 8, LANES), f32),
            pltpu.VMEM((10, 8, LANES), f32),
        ],
        name="finish",
    )(anchor, displacement, rim_weight, parent_field, nest_field, feedback_weight, *crossed)


VARIANTS = tuple(range(32))


def solution(mesh):
    in_specs = (P("px", "py", None), P("px", "py", None), P(), P(), P(), P())
    out_specs = (P("px", "py", None), P("px", "py", None))
    return jax.shard_map(local, mesh=mesh, in_specs=in_specs, out_specs=out_specs, check_vma=False)
```

```python
import functools

import jax
import jax.numpy as jnp
from jax import lax
from jax.experimental import pallas as pl
from jax.experimental.pallas import tpu as pltpu
from jax.sharding import PartitionSpec as P

REFINE = 3
TILE = 24
BLOCK = 8
LANES = 128
CHUNKS = 5
CHAN = CHUNKS * LANES
RIM_CELLS = 3
MARGIN = 2 * REFINE
NX, NY = 8, 16
FOOT_X, FOOT_Y = NX * BLOCK, NY * BLOCK
FINE_X, FINE_Y = NX * TILE, NY * TILE
PAD = 16
WINDOW_ORDER = ((0, 0), (0, 1), (0, 2), (1, 1), (1, 2))
TOP = 125
MESH = pl.DeviceIdType.MESH
TAPS = ((1 / 3, 2 / 3, 0.0), (0.0, 1.0, 0.0), (0.0, 2 / 3, 1 / 3))


def combine(taps, values):
    total = None
    for tap, value in zip(taps, values):
        if tap == 0.0:
            continue
        term = value if tap == 1.0 else tap * value
        total = term if total is None else total + term
    return total


class Dim:
    def __init__(self, count, q, low, high):
        self.count, self.q, self.low, self.high = count, q, low, high
        self.fixed = low == high
        self.second_from = 2 if BLOCK + high + 1 + 9 < TILE else 1
        first, last = BLOCK * q + low, BLOCK * q + high + 1
        self.near = sorted({first // TILE, (last + 2) // TILE})
        far = BLOCK * (count - 1) + 6
        self.far = sorted({(first + far) // TILE, (last + far + 3) // TILE})

    def split(self, index):
        g = index + self.q
        return lax.div(g, 3), lax.rem(g, 3)

    def used(self, index):
        return (3 * index + 2 >= self.q) & (3 * index - 1 - self.q < self.count)

    def strip_role(self, index):
        near, either, place = jnp.bool_(False), jnp.bool_(False), jnp.int32(0)
        for owners in (self.near, self.far):
            for order, owner in enumerate(owners):
                hit = index == owner
                either = either | hit
                if owners is self.near:
                    near = near | hit
                if order:
                    place = jnp.where(hit, order, place)
        return near, either, place


class Family:
    def __init__(self, sends, send, receives, receive, maybe_self=False):
        self.sends, self.send, self.receives, self.receive, self.maybe_self = sends, send, receives, receive, maybe_self


def each(count, body):
    if count == 1:
        body(jnp.int32(0))
    elif count:
        pl.loop(0, count)(body)


def send_kernel(
    dim_x, dim_y,
    anchor_ref, nest, parent_edges, parent_corners, average, send_x, send_y,
    arrived, nest_below, nest_beside, nest_corner, edges, corners, recv_x, recv_y,
    relay, compact,
    first_send, first_recv, next_send, next_recv, nest_send, nest_recv, edge_send, edge_recv, wx_send, wx_recv, wy_send, wy_recv,
):
    me_x, me_y = lax.axis_index("px"), lax.axis_index("py")

    def averages(dim, index, at, source, target, active, send_sem, recv_sem):
        owner, phase = dim.split(index)

        def source_of(slot):
            return 3 * index - 1 + slot - dim.q

        def valid(slot):
            return (source_of(slot) >= 0) & (source_of(slot) < dim.count) & dim.used(index)

        if not dim.fixed:
            return [Family(
                2, lambda i: (
                    active & ((i == 0) | (phase == 2)), at(owner + i), source(0, BLOCK),
                    target((phase + 1) * (1 - i), 0, BLOCK), send_sem.at[i], recv_sem.at[(phase + 1) * (1 - i)]),
                4, lambda i: (valid(i), at(source_of(i)), target(i, 0, BLOCK), recv_sem.at[i]), True)]
        cut = BLOCK - dim.low
        return [
            Family(
                1, lambda i: (
                    active & (phase < 2), at(owner), source(0, BLOCK), target(phase + 1, 0, BLOCK),
                    send_sem.at[0], recv_sem.at[phase + 1]),
                2, lambda i: (valid(i + 1), at(source_of(i + 1)), target(i + 1, 0, BLOCK), recv_sem.at[i + 1]), True),
            Family(
                1, lambda i: (
                    active & (phase == 2), at(owner), source(0, cut), target(3, 0, cut), send_sem.at[0], recv_sem.at[3]),
                1, lambda i: (valid(3), at(source_of(3)), target(3, 0, cut), recv_sem.at[3]), True),
            Family(
                1, lambda i: (
                    active & (phase == 2), at(owner + 1), source(cut, BLOCK - cut), target(0, cut, BLOCK - cut),
                    send_sem.at[1], recv_sem.at[0]),
                1, lambda i: (valid(0), at(source_of(0)), target(0, cut, BLOCK - cut), recv_sem.at[0]), True),
        ]

    always = me_x >= 0
    first = averages(
        dim_y, me_y, lambda y: (me_x, y), lambda start, size: average.at[:, pl.ds(start, size), :],
        lambda slot, start, size: relay.at[slot, :, pl.ds(start, size), :], always, first_send, first_recv)
    following = averages(
        dim_x, me_x, lambda x: (x, me_y), lambda start, size: compact.at[pl.ds(start, size)],
        lambda slot, start, size: arrived.at[slot, pl.ds(start, size)], dim_y.used(me_y), next_send, next_recv)
    for family in following:
        inner = family.receive
        family.receive = lambda i, inner=inner: (inner(i)[0] & dim_y.used(me_y), *inner(i)[1:])

    def inside(x, y):
        return (x >= 0) & (x < NX) & (y >= 0) & (y < NY)

    def shift(count, step, source, target, send_sem, recv_sem):
        def send(i):
            x, y = me_x + step(i)[0], me_y + step(i)[1]
            return inside(x, y), (x, y), source(i), target(i), send_sem(i), recv_sem(i)

        def receive(i):
            x, y = me_x - step(i)[0], me_y - step(i)[1]
            return inside(x, y), (x, y), target(i), recv_sem(i)

        return Family(count, send, count, receive)

    halos = []
    for order, (step_x, step_y) in enumerate(((1, 0), (0, 1), (1, 1))):
        rows, cols = (MARGIN if step_x else TILE), (MARGIN if step_y else TILE)
        lands = (nest_below, nest_beside, nest_corner)[order].at[:, pl.ds(0, cols), :]
        halos.append(shift(
            1, lambda i, step_x=step_x, step_y=step_y: (-step_x, -step_y),
            lambda i, rows=rows, cols=cols: nest.at[pl.ds(0, rows), pl.ds(0, cols), :], lambda i, lands=lands: lands,
            lambda i, order=order: nest_send.at[order], lambda i, order=order: nest_recv.at[order]))
    halos.append(shift(
        4, lambda i: (jnp.where(i < 2, 2 * i - 1, 0), jnp.where(i < 2, 0, 2 * i - 5)),
        lambda i: parent_edges.at[i], lambda i: edges.at[i], lambda i: edge_send.at[i], lambda i: edge_recv.at[i]))
    halos.append(shift(
        4, lambda i: (jnp.where(i < 2, -1, 1), 2 * i - jnp.where(i < 2, 1, 5)),
        lambda i: parent_corners.at[i], lambda i: corners.at[i], lambda i: edge_send.at[4 + i], lambda i: edge_recv.at[4 + i]))

    def windows(dim, index, along, along_index, swap, source, target, send_sem, recv_sem):
        near, strip, place = dim.strip_role(index)
        device = (lambda a, b: (b, a)) if swap else (lambda a, b: (a, b))
        places = max(len(dim.near), len(dim.far))
        owner, phase = along.split(along_index)

        def send(tail, i):
            second = jnp.where(i >= (2 if tail else 3), 1, 0)
            aim = i - second
            to = 3 * (along_index - second) + aim - along.q
            has = strip & (to >= 0) & (to < along.count)
            if tail and along.second_from == 2:
                has = has & (i != 2)
            return (
                has, device(jnp.where(near, 0, dim.count - 1), to), source(tail, i + second), target(tail, place, second),
                send_sem.at[tail, i], recv_sem.at[tail, place, second])

        def receive(tail, i):
            at = jnp.where(i >= 2, 1, 0)
            second = i - 2 * at
            across = jnp.int32(-1)
            for order in range(places):
                here_near = dim.near[order] if order < len(dim.near) else -1
                here_far = dim.far[order] if order < len(dim.far) else -1
                across = jnp.where(at == order, jnp.where(index == 0, here_near, here_far), across)
            has = ((index == 0) | (index == dim.count - 1)) & (across >= 0)
            if tail:
                has = has & (((second == 0) & (phase < 2)) | ((second == 1) & (phase >= along.second_from)))
            else:
                has = has & ((second == 0) | (phase == 2))
            has = has & (owner + second < along.count)
            return has, device(across, owner + second), target(tail, at, second), recv_sem.at[tail, at, second]

        return [
            Family(4, functools.partial(send, tail), 2 * places, functools.partial(receive, tail), True) for tail in (0, 1)
        ]

    part = (pl.ds(0, 8), pl.ds(8, 2))
    rims = windows(
        dim_x, me_x, dim_y, me_y, False, lambda tail, i: send_x.at[i, :, part[tail], :],
        lambda tail, place, second: recv_x.at[place, second, :, part[tail], :], wx_send, wx_recv)
    rims += windows(
        dim_y, me_y, dim_x, me_x, True, lambda tail, i: send_y.at[i, part[tail], pl.ds(0, 4), :],
        lambda tail, place, second: recv_y.at[place, second, part[tail], pl.ds(0, 4), :], wy_send, wy_recv)
    families = first + rims + following + halos

    def is_me(device):
        return (device[0] == me_x) & (device[1] == me_y)

    barrier = pltpu.get_barrier_semaphore()
    for family in families:
        def tell(i):
            has, device, _, _ = family.receive(i)

            @pl.when(has & jnp.logical_not(is_me(device)))
            def _():
                pl.semaphore_signal(barrier, inc=1, device_id=device, device_id_type=MESH)

        each(family.receives, tell)

    expected = jnp.int32(0)
    for family in families:
        def expect(i, count):
            has, device, *_ = family.send(i)
            return count + jnp.where(has & jnp.logical_not(is_me(device)), 1, 0)

        if family.sends == 1:
            expected = expect(jnp.int32(0), expected)
        else:
            expected = lax.fori_loop(0, family.sends, expect, expected)
    pl.semaphore_wait(barrier, expected)

    def remote(entry):
        _, device, src, dst, send_sem, recv_sem = entry
        return pltpu.make_async_remote_copy(
            src_ref=src, dst_ref=dst, send_sem=send_sem, recv_sem=recv_sem, device_id=device, device_id_type=MESH)

    def start(family):
        def body(i):
            entry = family.send(i)
            own = is_me(entry[1])

            @pl.when(entry[0] & jnp.logical_not(own))
            def _():
                remote(entry).start()

            if family.maybe_self:
                @pl.when(entry[0] & own)
                def _():
                    pltpu.make_async_copy(entry[2], entry[3], entry[5]).start()

        each(family.sends, body)

    def finish(family):
        def body(i):
            has, _, dst, recv_sem = family.receive(i)

            @pl.when(has)
            def _():
                pltpu.make_async_copy(dst, dst, recv_sem).wait()

        each(family.receives, body)

    def drain(family):
        def body(i):
            entry = family.send(i)

            @pl.when(entry[0] & jnp.logical_not(is_me(entry[1])))
            def _():
                remote(entry).wait_send()

        each(family.sends, body)

    for family in first + rims + halos:
        start(family)
    for family in first:
        finish(family)

    @pl.when(dim_y.used(me_y))
    def _():
        phase_y = anchor_ref[1] - BLOCK * dim_y.q

        @pl.loop(0, BLOCK)
        def _(row):
            whole = jnp.concatenate([relay[slot, row] for slot in range(4)], axis=0)
            compact[row] = pltpu.roll(whole, 3 * BLOCK + phase_y, 0)[:TILE]

    for family in following:
        start(family)
    for family in rims + halos + following:
        finish(family)
    for family in families:
        drain(family)


CROSSED = (
    (4, BLOCK, TILE), (MARGIN, TILE), (TILE, 8), (MARGIN, 8), (4, TILE), (4, 8), (2, 2, 4, 16), (2, 2, 10, 8),
)


def free(count, q):
    return Dim(count, q, max(0, 1 - BLOCK * q), min(BLOCK - 1, TOP - 1 - BLOCK * q))


def variant(order):
    if order < 16:
        dims = Dim(NX, TOP // BLOCK, TOP % BLOCK, TOP % BLOCK), free(NY, order)
    else:
        dims = free(NX, order - 16), Dim(NY, TOP // BLOCK, TOP % BLOCK, TOP % BLOCK)
    dma = pltpu.SemaphoreType.DMA
    hbm = pl.BlockSpec(memory_space=pl.ANY)
    return pl.pallas_call(
        functools.partial(send_kernel, *dims),
        name=f"send_{order}",
        out_shape=tuple(jax.ShapeDtypeStruct((*dims, CHAN), jnp.float32) for dims in CROSSED),
        in_specs=[pl.BlockSpec(memory_space=pltpu.SMEM)] + [hbm] * 6,
        out_specs=(hbm,) * len(CROSSED),
        scratch_shapes=[
            pltpu.VMEM((4, BLOCK, BLOCK, CHAN), jnp.float32), pltpu.VMEM((BLOCK, TILE, CHAN), jnp.float32),
            dma((2,)), dma((4,)), dma((2,)), dma((4,)), dma((3,)), dma((3,)), dma((8,)), dma((8,)),
            dma((2, 4)), dma((2, 2, 2)), dma((2, 4)), dma((2, 2, 2)),
        ],
        compiler_params=pltpu.CompilerParams(collective_id=order, has_side_effects=True),
    )


def facts_of(anchor_ref, move_ref):
    move = move_ref[0], move_ref[1]
    anchor = anchor_ref[0], anchor_ref[1]
    corner = anchor[0] + move[0], anchor[1] + move[1]
    q = lax.div(anchor[0], BLOCK), lax.div(anchor[1], BLOCK)
    phase = anchor[0] - BLOCK * q[0], anchor[1] - BLOCK * q[1]
    return move, corner, q, phase


def blender(rim_ref):
    rims = [rim_ref[level] for level in range(RIM_CELLS)]

    def blend_of(distance):
        value = jnp.where(distance == 2, rims[2], 0.0)
        value = jnp.where(distance == 1, rims[1], value)
        return jnp.where(distance == 0, rims[0], value)

    return blend_of


def iota(rows):
    return lax.broadcasted_iota(jnp.int32, (rows, LANES), 0)


def lanes_of(chunk):
    return pl.ds(pl.multiple_of(LANES * chunk, LANES), LANES)


def prepare_kernel(
    anchor_ref, move_ref, rim_ref, nest_ref, parent_ref, average, send_x, send_y, edges, corners, route,
    nest_all, padded_all, keep, load_sem,
):
    def load(order, chunk):
        if order == 0:
            return pltpu.make_async_copy(nest_ref.at[:, :, lanes_of(chunk)], nest_all.at[chunk], load_sem.at[order, chunk])
        return pltpu.make_async_copy(
            parent_ref.at[:, :, lanes_of(chunk)], padded_all.at[chunk, :, pl.ds(PAD, TILE), :], load_sem.at[order, chunk])

    for order in range(2):
        @pl.loop(0, CHUNKS)
        def _(chunk):
            load(order, chunk).start()

    me_x, me_y = lax.axis_index("px"), lax.axis_index("py")
    (move_x, move_y), (corner_x, corner_y), _, (phase_x, phase_y) = facts_of(anchor_ref, move_ref)
    blend_of = blender(rim_ref)
    order = jnp.where(anchor_ref[0] == TOP, lax.div(anchor_ref[1], BLOCK), 16 + lax.div(anchor_ref[0], BLOCK))
    route[0] = order

    @pl.loop(0, BLOCK, unroll=2)
    def _(k):
        row = REFINE * (BLOCK * me_x + k - move_x)
        col = REFINE * (BLOCK * me_y + iota(BLOCK) - move_y)
        for ii in range(3):
            for jj in range(3):
                keep[k, 3 * ii + jj] = (1.0 - blend_of(jnp.minimum(col + jj, row + ii))) * (1.0 / 9.0)

    def strip(corner, foot, me):
        first = corner - 1 - TILE * me
        near = (first <= TILE - 1) & (first + 2 >= 0)
        far = (first + foot - 2 <= TILE - 1) & (first + foot + 1 >= 0)
        return near | far, first + jnp.where(near, 0, foot - 2)

    strip_x, first_row = strip(corner_x, FOOT_X, me_x)
    strip_y, first_col = strip(corner_y, FOOT_Y, me_y)

    @pl.loop(0, CHUNKS)
    def _(chunk):
        lanes = lanes_of(chunk)
        load(0, chunk).wait()

        @pl.loop(0, BLOCK, unroll=4)
        def _(k):
            total = None
            for ii in range(3):
                for jj in range(3):
                    term = keep[k, 3 * ii + jj] * nest_all[chunk, REFINE * k + ii, pl.ds(jj, BLOCK, stride=REFINE), :]
                    total = term if total is None else total + term
            average[k, :, lanes] = total

    @pl.loop(0, CHUNKS)
    def _(chunk):
        lanes = lanes_of(chunk)
        load(1, chunk).wait()
        for side in range(2):
            edges[side, :, lanes] = padded_all[chunk, side * (TILE - 1), pl.ds(PAD, TILE), :]
        for row in range(TILE):
            for side in range(2):
                col = PAD + side * (TILE - 1)
                edges[2 + side, row:row + 1, lanes] = padded_all[chunk, row, col:col + 1, :]
        for order in range(4):
            row, col = order // 2 * (TILE - 1), PAD + order % 2 * (TILE - 1)
            corners[order, 0:1, lanes] = padded_all[chunk, row, col:col + 1, :]

        @pl.when(strip_x)
        def _():
            for order, (second, phase) in enumerate(WINDOW_ORDER):
                start = jnp.clip(PAD + BLOCK * phase - TILE * second + phase_y + move_y - 1, 0, TILE + PAD)
                for m in range(4):
                    send_x[order, m, :, lanes] = padded_all[chunk, jnp.clip(first_row + m, 0, TILE - 1), pl.ds(start, 16, stride=1), :]

        @pl.when(strip_y)
        def _():
            start = jnp.clip(PAD + first_col, 0, TILE + PAD)
            for order, (second, phase) in enumerate(WINDOW_ORDER):
                first = BLOCK * phase - TILE * second + phase_x + move_x - 1
                for m in range(10):
                    send_y[order, m, :, lanes] = padded_all[chunk, jnp.clip(first + m, 0, TILE - 1), pl.ds(start, 8, stride=1), :]


def finish_kernel(
    anchor_ref, move_ref, rim_ref, feed,
    parent_ref, nest_ref, arrived_ref, below_ref, beside_ref, corner_ref, edges_ref, corners_ref, recv_x_ref, recv_y_ref,
    parent_out, nest_out,
    wide_nest_all, wide_parent_all, arrived_all, edges_all, corners_all, recv_x_all, recv_y_all, nest_new_all, parent_new_all,
    feeds, placed, coefs, merged_x, fine_x, merged_y, fine_y, load_sem, store_sem,
):
    me_x, me_y = lax.axis_index("px"), lax.axis_index("py")
    (move_x, move_y), (corner_x, corner_y), (q_x, q_y), (phase_x, phase_y) = facts_of(anchor_ref, move_ref)
    blend_of = blender(rim_ref)
    first_k, first_l = TILE * me_x - corner_x, TILE * me_y - corner_y
    touched = (first_k < FOOT_X) & (first_k + TILE > 0) & (first_l < FOOT_Y) & (first_l + TILE > 0)
    edge_x, edge_y = (me_x == 0) | (me_x == NX - 1), (me_y == 0) | (me_y == NY - 1)
    always = me_x >= 0
    near_row = (first_k <= 0) & (first_k + TILE > 0)
    near_col = (first_l <= 0) & (first_l + TILE > 0)
    far_row = (first_k < FOOT_X) & (first_k + TILE > FOOT_X - move_x)
    far_col = (first_l < FOOT_Y) & (first_l + TILE > FOOT_Y - move_y)
    ring = touched & (near_row | near_col | far_row | far_col)
    inner = pl.ds(0, TILE)
    loads = (
        (always, nest_ref, lambda chunk: wide_nest_all.at[chunk, inner, inner, :]),
        (always, beside_ref, lambda chunk: wide_nest_all.at[chunk, inner, pl.ds(TILE, 8), :]),
        (always, below_ref, lambda chunk: wide_nest_all.at[chunk, pl.ds(TILE, MARGIN), inner, :]),
        (always, corner_ref, lambda chunk: wide_nest_all.at[chunk, pl.ds(TILE, MARGIN), pl.ds(TILE, 8), :]),
        (edge_x, recv_x_ref, lambda chunk: recv_x_all.at[chunk]),
        (edge_y, recv_y_ref, lambda chunk: recv_y_all.at[chunk]),
        (always, parent_ref, lambda chunk: wide_parent_all.at[chunk, pl.ds(1, TILE), pl.ds(8, TILE), :]),
        (touched, arrived_ref, lambda chunk: arrived_all.at[chunk]),
        (ring, edges_ref, lambda chunk: edges_all.at[chunk]),
        (ring, corners_ref, lambda chunk: corners_all.at[chunk]),
    )

    def load(order, chunk):
        _, source, target = loads[order]
        before = (slice(None),) * (len(source.shape) - 1)
        return pltpu.make_async_copy(source.at[(*before, lanes_of(chunk))], target(chunk), load_sem.at[order, chunk])

    def fetch(orders, chunk, act):
        for order in orders:
            if loads[order][0] is always:
                act(load(order, chunk))
            else:
                @pl.when(loads[order][0])
                def _():
                    act(load(order, chunk))

    @pl.loop(0, CHUNKS)
    def _(chunk):
        fetch(range(len(loads)), chunk, lambda copy: copy.start())

    def store(order, chunk):
        source, target = ((nest_new_all, nest_out), (parent_new_all, parent_out))[order]
        return pltpu.make_async_copy(source.at[chunk], target.at[:, :, lanes_of(chunk)], store_sem.at[order, chunk])

    for chunk in range(CHUNKS):
        feeds[chunk] = feed[pl.ds(LANES * chunk, LANES)].reshape(1, LANES)

    def weigh(row, tile, place):
        cols = first_l + BLOCK * tile + iota(BLOCK)
        k = first_k + row
        entered = (cols >= FOOT_Y - move_y) | (cols * 0 + k >= FOOT_X - move_x)
        partial = []
        for ii in range(3):
            weights = [
                jnp.where(entered, 1.0, blend_of(jnp.minimum(REFINE * cols + jj, REFINE * k + ii)))
                for jj in range(3)
            ]
            partial.append([combine([TAPS[jj][n] for jj in range(3)], weights) for n in range(3)])
        for m in range(3):
            for n in range(3):
                coefs[place, 3 * m + n] = combine(
                    [TAPS[ii][m] for ii in range(3)], [partial[ii][n] for ii in range(3)]) * (1.0 / 9.0)

    def fix_rows(first, count, work):
        @pl.loop(jnp.maximum(first, 0), jnp.minimum(first + count, TILE))
        def _(row):
            for tile in range(3):
                work(row, tile, 3 * row + tile)

    def fix_cols(first, count, work):
        low = lax.div(jnp.maximum(first, 0), BLOCK)
        high = lax.div(jnp.minimum(first + count, TILE) - 1, BLOCK) + 1

        @pl.loop(low, high)
        def _(tile):
            @pl.loop(0, TILE, unroll=4)
            def _(row):
                work(row, tile, 3 * row + tile)

    def along_ring(work):
        for touches, fixer, first, count in (
            (near_row, fix_rows, -first_k, 1), (far_row, fix_rows, FOOT_X - move_x - first_k, move_x),
            (near_col, fix_cols, -first_l, 1), (far_col, fix_cols, FOOT_Y - move_y - first_l, move_y),
        ):
            @pl.when(touched & touches)
            def _():
                fixer(first, count, work)

    along_ring(weigh)

    @pl.loop(0, CHUNKS)
    def _(chunk):
        wide_nest, wide_parent, arrived = wide_nest_all.at[chunk], wide_parent_all.at[chunk], arrived_all.at[chunk]
        edges, corners, recv_x, recv_y = edges_all.at[chunk], corners_all.at[chunk], recv_x_all.at[chunk], recv_y_all.at[chunk]
        nest_new, parent_new = nest_new_all.at[chunk], parent_new_all.at[chunk]
        fetch(range(6), chunk, lambda copy: copy.wait())

        @pl.loop(0, TILE, unroll=8)
        def _(row):
            nest_new[row] = wide_nest[row + REFINE * move_x, pl.ds(REFINE * move_y, TILE, stride=1), :]

        def blended(row, cols, shifted, interp):
            entered = (cols >= FINE_Y - REFINE * move_y) | (cols * 0 + row >= FINE_X - REFINE * move_x)
            moved = jnp.where(entered, interp, shifted)
            distance = jnp.minimum(jnp.minimum(cols, FINE_Y - 1 - cols), jnp.minimum(row, FINE_X - 1 - row))
            return moved + blend_of(distance) * (interp - moved)

        def edge_columns(at_near):
            rel_row = BLOCK * lax.rem(me_x + q_x, 3) + phase_x + move_x - 1
            columns = iota(BLOCK)
            if at_near:
                first_col, step, bound, base = 0, columns, TILE * (lax.div(q_y, 3) + 1), corner_y - 1
            else:
                first_col, step = TILE - BLOCK, columns - 2
                bound, base = TILE * (lax.div(q_y + NY - 1, 3) + 1), corner_y - 1 + FOOT_Y - 2
            beyond = base + columns >= bound
            cell = jnp.where(step >= 3, 1, 0)
            sub = step - 3 * cell
            taps = []
            for n in range(3 if at_near else 4):
                m = n - cell
                left = jnp.where(m == 0, 1 / 3, jnp.where(m == 1, 2 / 3, 0.0))
                mid = jnp.where(m == 1, 1.0, 0.0)
                right = jnp.where(m == 1, 2 / 3, jnp.where(m == 2, 1 / 3, 0.0))
                taps.append(jnp.where(sub == 0, left, jnp.where(sub == 1, mid, right)))
            in_strip = (step >= 0) & (step < (3 if at_near else 6))
            for m in range(10):
                second = jnp.where(rel_row + m >= TILE, 1, 0)
                merged_y[m] = jnp.where(beyond, recv_y[1, second, m], recv_y[0, second, m])
                total = None
                for n, tap in enumerate(taps):
                    term = tap * jnp.broadcast_to(merged_y[m, n:n + 1, :], (BLOCK, LANES))
                    total = term if total is None else total + term
                fine_y[m] = total

            @pl.loop(0, BLOCK, unroll=4)
            def _(k):
                for ii in range(3):
                    row = REFINE * k + ii
                    interp = combine(TAPS[ii], [fine_y[k + m] for m in range(3)])
                    shifted = wide_nest[row + REFINE * move_x, pl.ds(first_col + REFINE * move_y, BLOCK, stride=1), :]
                    value = blended(TILE * me_x + row, TILE * me_y + first_col + columns, shifted, interp)
                    nest_new[row, pl.ds(first_col, BLOCK), :] = jnp.where(in_strip, value, shifted)

        def edge_rows(at_near):
            rel_col = BLOCK * lax.rem(me_y + q_y, 3) + phase_y + move_y - 1
            second = rel_col + iota(16) >= TILE
            cols = TILE * me_y + iota(TILE)
            if at_near:
                bound, first_row, cells = TILE * (lax.div(q_x, 3) + 1), corner_x - 1, 1
            else:
                bound, first_row, cells = TILE * (lax.div(q_x + NX - 1, 3) + 1), corner_x - 1 + FOOT_X - 2, 2
            for m in range(cells + 2):
                place = jnp.where(first_row + m >= bound, 1, 0)
                merged_x[...] = jnp.where(second, recv_x[place, 1, m], recv_x[place, 0, m])
                for jj in range(3):
                    fine_x[m, pl.ds(jj, BLOCK, stride=REFINE), :] = combine(
                        TAPS[jj], [merged_x[pl.ds(n, BLOCK), :] for n in range(3)])
            for k in range(cells):
                for ii in range(3):
                    row = (0 if at_near else TILE - 3 * cells) + 3 * k + ii
                    interp = combine(TAPS[ii], [fine_x[k + m] for m in range(3)])
                    shifted = wide_nest[row + REFINE * move_x, pl.ds(REFINE * move_y, TILE, stride=1), :]
                    nest_new[row] = blended(TILE * me_x + row, cols, shifted, interp)

        for at_near in (True, False):
            @pl.when(me_y == (0 if at_near else NY - 1))
            def _():
                edge_columns(at_near)
        for at_near in (True, False):
            @pl.when(me_x == (0 if at_near else NX - 1))
            def _():
                edge_rows(at_near)

        store(0, chunk).start()
        fetch(range(6, len(loads)), chunk, lambda copy: copy.wait())

        @pl.when(jnp.logical_not(touched))
        def _():
            parent_new[...] = wide_parent[pl.ds(1, TILE), pl.ds(8, TILE), :]

        @pl.when(touched)
        def _():
            l = first_l + iota(TILE)
            weight = feeds[chunk]

            @pl.loop(0, TILE, unroll=8)
            def _(row):
                k = l * 0 + (first_k + row)
                covered = (l >= 0) & (l < FOOT_Y) & (k >= 0) & (k < FOOT_X)
                usable = covered & (l < FOOT_Y - move_y) & (k < FOOT_X - move_x)
                at = row + BLOCK - phase_x
                slot_x, in_x = lax.div(at, BLOCK), lax.rem(at, BLOCK)
                whole = jnp.where(usable, arrived[slot_x, in_x], 0.0)
                own = wide_parent[row + 1, pl.ds(8, TILE), :]
                placed[row] = whole
                parent_new[row] = jnp.where(covered, own + weight * (whole - own), own)

            @pl.when(near_row | near_col | far_row | far_col)
            def _():
                for row in range(TILE):
                    wide_parent[row + 1, pl.ds(7, 1), :] = edges[3, row:row + 1, :]
                    wide_parent[row + 1, pl.ds(8 + TILE, 1), :] = edges[2, row:row + 1, :]
                for down, row in ((1, 0), (0, TILE + 1)):
                    wide_parent[row, pl.ds(8, TILE), :] = edges[down]
                    wide_parent[row, pl.ds(7, 1), :] = corners[2 * down + 1, 0:1, :]
                    wide_parent[row, pl.ds(8 + TILE, 1), :] = corners[2 * down, 0:1, :]

                def fix(row, tile, place):
                    cols = first_l + BLOCK * tile + iota(BLOCK)
                    k = first_k + row
                    total = placed[row, pl.ds(pl.multiple_of(BLOCK * tile, BLOCK), BLOCK), :]
                    for m in range(3):
                        for n in range(3):
                            total = total + coefs[place, 3 * m + n] * wide_parent[row + m, pl.ds(7 + BLOCK * tile + n, BLOCK, stride=1), :]
                    covered = (cols >= 0) & (cols < FOOT_Y) & (cols * 0 + k >= 0) & (cols * 0 + k < FOOT_X)
                    own = wide_parent[row + 1, pl.ds(pl.multiple_of(8 + BLOCK * tile, BLOCK), BLOCK), :]
                    parent_new[row, pl.ds(pl.multiple_of(BLOCK * tile, BLOCK), BLOCK), :] = jnp.where(
                        covered, own + weight * (total - own), own)

                along_ring(fix)

        store(1, chunk).start()

    @pl.loop(0, CHUNKS)
    def _(chunk):
        store(0, chunk).wait()
        store(1, chunk).wait()


def local(parent_field, nest_field, anchor, displacement, feedback_weight, rim_weight):
    f32, dma = jnp.float32, pltpu.SemaphoreType.DMA
    smem, hbm, vmem = (pl.BlockSpec(memory_space=space) for space in (pltpu.SMEM, pl.ANY, pltpu.VMEM))
    prepared = ((BLOCK, BLOCK), (5, 4, 16), (5, 10, 8), (4, TILE), (4, 8))
    average, send_x, send_y, parent_edges, parent_corners, route = pl.pallas_call(
        prepare_kernel,
        out_shape=(
            *(jax.ShapeDtypeStruct((*dims, CHAN), f32) for dims in prepared), jax.ShapeDtypeStruct((1,), jnp.int32)),
        in_specs=[smem, smem, smem, hbm, hbm],
        out_specs=(*(vmem for _ in prepared), smem),
        scratch_shapes=[
            pltpu.VMEM((CHUNKS, TILE, TILE, LANES), f32), pltpu.VMEM((CHUNKS, TILE, TILE + 2 * PAD, LANES), f32),
            pltpu.VMEM((BLOCK, 9, BLOCK, LANES), f32), dma((2, CHUNKS)),
        ],
        name="prepare",
    )(anchor, displacement, rim_weight, nest_field, parent_field)
    crossed = lax.switch(
        route[0], [variant(v) for v in VARIANTS], anchor, nest_field, parent_edges, parent_corners, average, send_x, send_y)
    shape = jax.ShapeDtypeStruct((TILE, TILE, CHAN), f32)
    chunked = (
        (TILE + MARGIN, TILE + 8), (TILE + 2, TILE + 16), (4, BLOCK, TILE), (4, TILE), (4, 8), (2, 2, 4, 16), (2, 2, 10, 8),
        (TILE, TILE), (TILE, TILE),
    )
    return pl.pallas_call(
        finish_kernel,
        out_shape=(shape, shape),
        in_specs=[smem, smem, smem, vmem, *([hbm] * 10)],
        out_specs=(hbm, hbm),
        scratch_shapes=[
            *(pltpu.VMEM((CHUNKS, *dims, LANES), f32) for dims in chunked),
            pltpu.VMEM((CHUNKS, 1, LANES), f32),
            pltpu.VMEM((TILE, TILE, LANES), f32),
            pltpu.VMEM((3 * TILE, 9, BLOCK, LANES), f32),
            pltpu.VMEM((16, LANES), f32),
            pltpu.VMEM((4, TILE, LANES), f32),
            pltpu.VMEM((10, 8, LANES), f32),
            pltpu.VMEM((10, 8, LANES), f32),
            dma((10, CHUNKS)), dma((2, CHUNKS)),
        ],
        name="finish",
    )(anchor, displacement, rim_weight, feedback_weight, parent_field, nest_field, *crossed)


VARIANTS = tuple(range(32))


def solution(mesh):
    in_specs = (P("px", "py", None), P("px", "py", None), P(), P(), P(), P())
    out_specs = (P("px", "py", None), P("px", "py", None))
    return jax.shard_map(local, mesh=mesh, in_specs=in_specs, out_specs=out_specs, check_vma=False)
```

```python
import functools

import jax
import jax.numpy as jnp
from jax import lax
from jax.experimental import pallas as pl
from jax.experimental.pallas import tpu as pltpu
from jax.sharding import PartitionSpec as P

REFINE = 3
TILE = 24
BLOCK = 8
LANES = 128
CHUNKS = 5
CHAN = CHUNKS * LANES
RIM_CELLS = 3
MARGIN = 2 * REFINE
NX, NY = 8, 16
FOOT_X, FOOT_Y = NX * BLOCK, NY * BLOCK
FINE_X, FINE_Y = NX * TILE, NY * TILE
PAD = 16
WINDOW_ORDER = ((0, 0), (0, 1), (0, 2), (1, 1), (1, 2))
TOP = 125
MESH = pl.DeviceIdType.MESH
TAPS = ((1 / 3, 2 / 3, 0.0), (0.0, 1.0, 0.0), (0.0, 2 / 3, 1 / 3))


def combine(taps, values):
    total = None
    for tap, value in zip(taps, values):
        if tap == 0.0:
            continue
        term = value if tap == 1.0 else tap * value
        total = term if total is None else total + term
    return total


class Dim:
    def __init__(self, count, q, low, high):
        self.count, self.q, self.low, self.high = count, q, low, high
        self.fixed = low == high
        self.second_from = 2 if BLOCK + high + 1 + 9 < TILE else 1
        first, last = BLOCK * q + low, BLOCK * q + high + 1
        self.near = sorted({first // TILE, (last + 2) // TILE})
        far = BLOCK * (count - 1) + 6
        self.far = sorted({(first + far) // TILE, (last + far + 3) // TILE})

    def split(self, index):
        g = index + self.q
        return lax.div(g, 3), lax.rem(g, 3)

    def used(self, index):
        return (3 * index + 2 >= self.q) & (3 * index - 1 - self.q < self.count)

    def strip_role(self, index):
        near, either, place = jnp.bool_(False), jnp.bool_(False), jnp.int32(0)
        for owners in (self.near, self.far):
            for order, owner in enumerate(owners):
                hit = index == owner
                either = either | hit
                if owners is self.near:
                    near = near | hit
                if order:
                    place = jnp.where(hit, order, place)
        return near, either, place


class Family:
    def __init__(self, sends, send, receives, receive, maybe_self=False):
        self.sends, self.send, self.receives, self.receive, self.maybe_self = sends, send, receives, receive, maybe_self


def each(count, body):
    if count == 1:
        body(jnp.int32(0))
    elif count:
        pl.loop(0, count)(body)


def send_kernel(
    dim_x, dim_y,
    anchor_ref, nest, parent_edges, parent_corners, average, send_x, send_y,
    arrived, nest_below, nest_beside, nest_corner, edges, corners, recv_x, recv_y,
    relay, compact,
    first_send, first_recv, next_send, next_recv, nest_send, nest_recv, edge_send, edge_recv, wx_send, wx_recv, wy_send, wy_recv,
):
    me_x, me_y = lax.axis_index("px"), lax.axis_index("py")

    def averages(dim, index, at, source, target, active, send_sem, recv_sem):
        owner, phase = dim.split(index)

        def source_of(slot):
            return 3 * index - 1 + slot - dim.q

        def valid(slot):
            return (source_of(slot) >= 0) & (source_of(slot) < dim.count) & dim.used(index)

        if not dim.fixed:
            return [Family(
                2, lambda i: (
                    active & ((i == 0) | (phase == 2)), at(owner + i), source(0, BLOCK),
                    target((phase + 1) * (1 - i), 0, BLOCK), send_sem.at[i], recv_sem.at[(phase + 1) * (1 - i)]),
                4, lambda i: (valid(i), at(source_of(i)), target(i, 0, BLOCK), recv_sem.at[i]), True)]
        cut = BLOCK - dim.low
        return [
            Family(
                1, lambda i: (
                    active & (phase < 2), at(owner), source(0, BLOCK), target(phase + 1, 0, BLOCK),
                    send_sem.at[0], recv_sem.at[phase + 1]),
                2, lambda i: (valid(i + 1), at(source_of(i + 1)), target(i + 1, 0, BLOCK), recv_sem.at[i + 1]), True),
            Family(
                1, lambda i: (
                    active & (phase == 2), at(owner), source(0, cut), target(3, 0, cut), send_sem.at[0], recv_sem.at[3]),
                1, lambda i: (valid(3), at(source_of(3)), target(3, 0, cut), recv_sem.at[3]), True),
            Family(
                1, lambda i: (
                    active & (phase == 2), at(owner + 1), source(cut, BLOCK - cut), target(0, cut, BLOCK - cut),
                    send_sem.at[1], recv_sem.at[0]),
                1, lambda i: (valid(0), at(source_of(0)), target(0, cut, BLOCK - cut), recv_sem.at[0]), True),
        ]

    always = me_x >= 0
    first = averages(
        dim_y, me_y, lambda y: (me_x, y), lambda start, size: average.at[:, pl.ds(start, size), :],
        lambda slot, start, size: relay.at[slot, :, pl.ds(start, size), :], always, first_send, first_recv)
    following = averages(
        dim_x, me_x, lambda x: (x, me_y), lambda start, size: compact.at[pl.ds(start, size)],
        lambda slot, start, size: arrived.at[slot, pl.ds(start, size)], dim_y.used(me_y), next_send, next_recv)
    for family in following:
        inner = family.receive
        family.receive = lambda i, inner=inner: (inner(i)[0] & dim_y.used(me_y), *inner(i)[1:])

    def inside(x, y):
        return (x >= 0) & (x < NX) & (y >= 0) & (y < NY)

    def shift(count, step, source, target, send_sem, recv_sem):
        def send(i):
            x, y = me_x + step(i)[0], me_y + step(i)[1]
            return inside(x, y), (x, y), source(i), target(i), send_sem(i), recv_sem(i)

        def receive(i):
            x, y = me_x - step(i)[0], me_y - step(i)[1]
            return inside(x, y), (x, y), target(i), recv_sem(i)

        return Family(count, send, count, receive)

    halos = []
    for order, (step_x, step_y) in enumerate(((1, 0), (0, 1), (1, 1))):
        rows, cols = (MARGIN if step_x else TILE), (MARGIN if step_y else TILE)
        lands = (nest_below, nest_beside, nest_corner)[order].at[:, pl.ds(0, cols), :]
        halos.append(shift(
            1, lambda i, step_x=step_x, step_y=step_y: (-step_x, -step_y),
            lambda i, rows=rows, cols=cols: nest.at[pl.ds(0, rows), pl.ds(0, cols), :], lambda i, lands=lands: lands,
            lambda i, order=order: nest_send.at[order], lambda i, order=order: nest_recv.at[order]))
    halos.append(shift(
        4, lambda i: (jnp.where(i < 2, 2 * i - 1, 0), jnp.where(i < 2, 0, 2 * i - 5)),
        lambda i: parent_edges.at[i], lambda i: edges.at[i], lambda i: edge_send.at[i], lambda i: edge_recv.at[i]))
    halos.append(shift(
        4, lambda i: (jnp.where(i < 2, -1, 1), 2 * i - jnp.where(i < 2, 1, 5)),
        lambda i: parent_corners.at[i], lambda i: corners.at[i], lambda i: edge_send.at[4 + i], lambda i: edge_recv.at[4 + i]))

    def windows(dim, index, along, along_index, swap, source, target, send_sem, recv_sem):
        near, strip, place = dim.strip_role(index)
        device = (lambda a, b: (b, a)) if swap else (lambda a, b: (a, b))
        places = max(len(dim.near), len(dim.far))
        owner, phase = along.split(along_index)

        def send(tail, i):
            second = jnp.where(i >= (2 if tail else 3), 1, 0)
            aim = i - second
            to = 3 * (along_index - second) + aim - along.q
            has = strip & (to >= 0) & (to < along.count)
            if tail and along.second_from == 2:
                has = has & (i != 2)
            return (
                has, device(jnp.where(near, 0, dim.count - 1), to), source(tail, i + second), target(tail, place, second),
                send_sem.at[tail, i], recv_sem.at[tail, place, second])

        def receive(tail, i):
            at = jnp.where(i >= 2, 1, 0)
            second = i - 2 * at
            across = jnp.int32(-1)
            for order in range(places):
                here_near = dim.near[order] if order < len(dim.near) else -1
                here_far = dim.far[order] if order < len(dim.far) else -1
                across = jnp.where(at == order, jnp.where(index == 0, here_near, here_far), across)
            has = ((index == 0) | (index == dim.count - 1)) & (across >= 0)
            if tail:
                has = has & (((second == 0) & (phase < 2)) | ((second == 1) & (phase >= along.second_from)))
            else:
                has = has & ((second == 0) | (phase == 2))
            has = has & (owner + second < along.count)
            return has, device(across, owner + second), target(tail, at, second), recv_sem.at[tail, at, second]

        return [
            Family(4, functools.partial(send, tail), 2 * places, functools.partial(receive, tail), True) for tail in (0, 1)
        ]

    part = (pl.ds(0, 8), pl.ds(8, 2))
    rims = windows(
        dim_x, me_x, dim_y, me_y, False, lambda tail, i: send_x.at[i, :, part[tail], :],
        lambda tail, place, second: recv_x.at[place, second, :, part[tail], :], wx_send, wx_recv)
    rims += windows(
        dim_y, me_y, dim_x, me_x, True, lambda tail, i: send_y.at[i, part[tail], pl.ds(0, 4), :],
        lambda tail, place, second: recv_y.at[place, second, part[tail], pl.ds(0, 4), :], wy_send, wy_recv)
    families = first + rims + following + halos

    def is_me(device):
        return (device[0] == me_x) & (device[1] == me_y)

    barrier = pltpu.get_barrier_semaphore()
    for family in families:
        def tell(i):
            has, device, _, _ = family.receive(i)

            @pl.when(has & jnp.logical_not(is_me(device)))
            def _():
                pl.semaphore_signal(barrier, inc=1, device_id=device, device_id_type=MESH)

        each(family.receives, tell)

    expected = jnp.int32(0)
    for family in families:
        def expect(i, count):
            has, device, *_ = family.send(i)
            return count + jnp.where(has & jnp.logical_not(is_me(device)), 1, 0)

        if family.sends == 1:
            expected = expect(jnp.int32(0), expected)
        else:
            expected = lax.fori_loop(0, family.sends, expect, expected)
    pl.semaphore_wait(barrier, expected)

    def remote(entry):
        _, device, src, dst, send_sem, recv_sem = entry
        return pltpu.make_async_remote_copy(
            src_ref=src, dst_ref=dst, send_sem=send_sem, recv_sem=recv_sem, device_id=device, device_id_type=MESH)

    def start(family):
        def body(i):
            entry = family.send(i)
            own = is_me(entry[1])

            @pl.when(entry[0] & jnp.logical_not(own))
            def _():
                remote(entry).start()

            if family.maybe_self:
                @pl.when(entry[0] & own)
                def _():
                    pltpu.make_async_copy(entry[2], entry[3], entry[5]).start()

        each(family.sends, body)

    def finish(family):
        def body(i):
            has, _, dst, recv_sem = family.receive(i)

            @pl.when(has)
            def _():
                pltpu.make_async_copy(dst, dst, recv_sem).wait()

        each(family.receives, body)

    def drain(family):
        def body(i):
            entry = family.send(i)

            @pl.when(entry[0] & jnp.logical_not(is_me(entry[1])))
            def _():
                remote(entry).wait_send()

        each(family.sends, body)

    for family in first + rims + halos[:1] + halos[2:]:
        start(family)
    for family in first:
        finish(family)

    @pl.when(dim_y.used(me_y))
    def _():
        phase_y = anchor_ref[1] - BLOCK * dim_y.q

        @pl.loop(0, BLOCK)
        def _(row):
            whole = jnp.concatenate([relay[slot, row] for slot in range(4)], axis=0)
            compact[row] = pltpu.roll(whole, 3 * BLOCK + phase_y, 0)[:TILE]

    for family in following + halos[1:2]:
        start(family)
    for family in rims + halos + following:
        finish(family)
    for family in families:
        drain(family)


CROSSED = (
    (4, BLOCK, TILE), (MARGIN, TILE), (TILE, 8), (MARGIN, 8), (4, TILE), (4, 8), (2, 2, 4, 16), (2, 2, 10, 8),
)


def free(count, q):
    return Dim(count, q, max(0, 1 - BLOCK * q), min(BLOCK - 1, TOP - 1 - BLOCK * q))


def variant(order):
    if order < 16:
        dims = Dim(NX, TOP // BLOCK, TOP % BLOCK, TOP % BLOCK), free(NY, order)
    else:
        dims = free(NX, order - 16), Dim(NY, TOP // BLOCK, TOP % BLOCK, TOP % BLOCK)
    dma = pltpu.SemaphoreType.DMA
    hbm = pl.BlockSpec(memory_space=pl.ANY)
    return pl.pallas_call(
        functools.partial(send_kernel, *dims),
        name=f"send_{order}",
        out_shape=tuple(jax.ShapeDtypeStruct((*dims, CHAN), jnp.float32) for dims in CROSSED),
        in_specs=[pl.BlockSpec(memory_space=pltpu.SMEM)] + [hbm] * 6,
        out_specs=(hbm,) * len(CROSSED),
        scratch_shapes=[
            pltpu.VMEM((4, BLOCK, BLOCK, CHAN), jnp.float32), pltpu.VMEM((BLOCK, TILE, CHAN), jnp.float32),
            dma((2,)), dma((4,)), dma((2,)), dma((4,)), dma((3,)), dma((3,)), dma((8,)), dma((8,)),
            dma((2, 4)), dma((2, 2, 2)), dma((2, 4)), dma((2, 2, 2)),
        ],
        compiler_params=pltpu.CompilerParams(collective_id=order, has_side_effects=True),
    )


def facts_of(anchor_ref, move_ref):
    move = move_ref[0], move_ref[1]
    anchor = anchor_ref[0], anchor_ref[1]
    corner = anchor[0] + move[0], anchor[1] + move[1]
    q = lax.div(anchor[0], BLOCK), lax.div(anchor[1], BLOCK)
    phase = anchor[0] - BLOCK * q[0], anchor[1] - BLOCK * q[1]
    return move, corner, q, phase


def blender(rim_ref):
    rims = [rim_ref[level] for level in range(RIM_CELLS)]

    def blend_of(distance):
        value = jnp.where(distance == 2, rims[2], 0.0)
        value = jnp.where(distance == 1, rims[1], value)
        return jnp.where(distance == 0, rims[0], value)

    return blend_of


def iota(rows):
    return lax.broadcasted_iota(jnp.int32, (rows, LANES), 0)


def lanes_of(chunk):
    return pl.ds(pl.multiple_of(LANES * chunk, LANES), LANES)


def prepare_kernel(
    anchor_ref, move_ref, rim_ref, nest_ref, parent_ref, average, send_x, send_y, edges, corners, route,
    nest_all, padded_all, keep, load_sem,
):
    def load(order, chunk):
        if order == 0:
            return pltpu.make_async_copy(nest_ref.at[:, :, lanes_of(chunk)], nest_all.at[chunk], load_sem.at[order, chunk])
        return pltpu.make_async_copy(
            parent_ref.at[:, :, lanes_of(chunk)], padded_all.at[chunk, :, pl.ds(PAD, TILE), :], load_sem.at[order, chunk])

    for order in range(2):
        @pl.loop(0, CHUNKS)
        def _(chunk):
            load(order, chunk).start()

    me_x, me_y = lax.axis_index("px"), lax.axis_index("py")
    (move_x, move_y), (corner_x, corner_y), _, (phase_x, phase_y) = facts_of(anchor_ref, move_ref)
    blend_of = blender(rim_ref)
    order = jnp.where(anchor_ref[0] == TOP, lax.div(anchor_ref[1], BLOCK), 16 + lax.div(anchor_ref[0], BLOCK))
    route[0] = order

    @pl.loop(0, BLOCK, unroll=2)
    def _(k):
        row = REFINE * (BLOCK * me_x + k - move_x)
        col = REFINE * (BLOCK * me_y + iota(BLOCK) - move_y)
        for ii in range(3):
            for jj in range(3):
                keep[k, 3 * ii + jj] = (1.0 - blend_of(jnp.minimum(col + jj, row + ii))) * (1.0 / 9.0)

    def strip(corner, foot, me):
        first = corner - 1 - TILE * me
        near = (first <= TILE - 1) & (first + 2 >= 0)
        far = (first + foot - 2 <= TILE - 1) & (first + foot + 1 >= 0)
        return near | far, first + jnp.where(near, 0, foot - 2)

    strip_x, first_row = strip(corner_x, FOOT_X, me_x)
    strip_y, first_col = strip(corner_y, FOOT_Y, me_y)

    @pl.loop(0, CHUNKS)
    def _(chunk):
        lanes = lanes_of(chunk)
        load(0, chunk).wait()

        @pl.loop(0, BLOCK, unroll=4)
        def _(k):
            total = None
            for ii in range(3):
                for jj in range(3):
                    term = keep[k, 3 * ii + jj] * nest_all[chunk, REFINE * k + ii, pl.ds(jj, BLOCK, stride=REFINE), :]
                    total = term if total is None else total + term
            average[k, :, lanes] = total

    @pl.loop(0, CHUNKS)
    def _(chunk):
        lanes = lanes_of(chunk)
        load(1, chunk).wait()
        for side in range(2):
            edges[side, :, lanes] = padded_all[chunk, side * (TILE - 1), pl.ds(PAD, TILE), :]
        for row in range(TILE):
            for side in range(2):
                col = PAD + side * (TILE - 1)
                edges[2 + side, row:row + 1, lanes] = padded_all[chunk, row, col:col + 1, :]
        for order in range(4):
            row, col = order // 2 * (TILE - 1), PAD + order % 2 * (TILE - 1)
            corners[order, 0:1, lanes] = padded_all[chunk, row, col:col + 1, :]

        @pl.when(strip_x)
        def _():
            for order, (second, phase) in enumerate(WINDOW_ORDER):
                start = jnp.clip(PAD + BLOCK * phase - TILE * second + phase_y + move_y - 1, 0, TILE + PAD)
                for m in range(4):
                    send_x[order, m, :, lanes] = padded_all[chunk, jnp.clip(first_row + m, 0, TILE - 1), pl.ds(start, 16, stride=1), :]

        @pl.when(strip_y)
        def _():
            start = jnp.clip(PAD + first_col, 0, TILE + PAD)
            for order, (second, phase) in enumerate(WINDOW_ORDER):
                first = BLOCK * phase - TILE * second + phase_x + move_x - 1
                for m in range(10):
                    send_y[order, m, :, lanes] = padded_all[chunk, jnp.clip(first + m, 0, TILE - 1), pl.ds(start, 8, stride=1), :]


def finish_kernel(
    anchor_ref, move_ref, rim_ref, feed,
    parent_ref, nest_ref, arrived_ref, below_ref, beside_ref, corner_ref, edges_ref, corners_ref, recv_x_ref, recv_y_ref,
    parent_out, nest_out,
    wide_nest_all, wide_parent_all, arrived_all, edges_all, corners_all, recv_x_all, recv_y_all, nest_new_all, parent_new_all,
    feeds, placed, coefs, merged_x, fine_x, merged_y, fine_y, load_sem, store_sem,
):
    me_x, me_y = lax.axis_index("px"), lax.axis_index("py")
    (move_x, move_y), (corner_x, corner_y), (q_x, q_y), (phase_x, phase_y) = facts_of(anchor_ref, move_ref)
    blend_of = blender(rim_ref)
    first_k, first_l = TILE * me_x - corner_x, TILE * me_y - corner_y
    touched = (first_k < FOOT_X) & (first_k + TILE > 0) & (first_l < FOOT_Y) & (first_l + TILE > 0)
    edge_x, edge_y = (me_x == 0) | (me_x == NX - 1), (me_y == 0) | (me_y == NY - 1)
    always = me_x >= 0
    near_row = (first_k <= 0) & (first_k + TILE > 0)
    near_col = (first_l <= 0) & (first_l + TILE > 0)
    far_row = (first_k < FOOT_X) & (first_k + TILE > FOOT_X - move_x)
    far_col = (first_l < FOOT_Y) & (first_l + TILE > FOOT_Y - move_y)
    ring = touched & (near_row | near_col | far_row | far_col)
    inner = pl.ds(0, TILE)
    loads = (
        (always, nest_ref, lambda chunk: wide_nest_all.at[chunk, inner, inner, :]),
        (always, beside_ref, lambda chunk: wide_nest_all.at[chunk, inner, pl.ds(TILE, 8), :]),
        (always, below_ref, lambda chunk: wide_nest_all.at[chunk, pl.ds(TILE, MARGIN), inner, :]),
        (always, corner_ref, lambda chunk: wide_nest_all.at[chunk, pl.ds(TILE, MARGIN), pl.ds(TILE, 8), :]),
        (edge_x, recv_x_ref, lambda chunk: recv_x_all.at[chunk]),
        (edge_y, recv_y_ref, lambda chunk: recv_y_all.at[chunk]),
        (always, parent_ref, lambda chunk: wide_parent_all.at[chunk, pl.ds(1, TILE), pl.ds(8, TILE), :]),
        (touched, arrived_ref, lambda chunk: arrived_all.at[chunk]),
        (ring, edges_ref, lambda chunk: edges_all.at[chunk]),
        (ring, corners_ref, lambda chunk: corners_all.at[chunk]),
    )

    def load(order, chunk):
        _, source, target = loads[order]
        before = (slice(None),) * (len(source.shape) - 1)
        return pltpu.make_async_copy(source.at[(*before, lanes_of(chunk))], target(chunk), load_sem.at[order, chunk])

    def fetch(orders, chunk, act):
        for order in orders:
            if loads[order][0] is always:
                act(load(order, chunk))
            else:
                @pl.when(loads[order][0])
                def _():
                    act(load(order, chunk))

    @pl.loop(0, CHUNKS)
    def _(chunk):
        fetch(range(len(loads)), chunk, lambda copy: copy.start())

    def store(order, chunk):
        source, target = ((nest_new_all, nest_out), (parent_new_all, parent_out))[order]
        return pltpu.make_async_copy(source.at[chunk], target.at[:, :, lanes_of(chunk)], store_sem.at[order, chunk])

    for chunk in range(CHUNKS):
        feeds[chunk] = feed[pl.ds(LANES * chunk, LANES)].reshape(1, LANES)

    def weigh(row, tile, place):
        cols = first_l + BLOCK * tile + iota(BLOCK)
        k = first_k + row
        entered = (cols >= FOOT_Y - move_y) | (cols * 0 + k >= FOOT_X - move_x)
        partial = []
        for ii in range(3):
            weights = [
                jnp.where(entered, 1.0, blend_of(jnp.minimum(REFINE * cols + jj, REFINE * k + ii)))
                for jj in range(3)
            ]
            partial.append([combine([TAPS[jj][n] for jj in range(3)], weights) for n in range(3)])
        for m in range(3):
            for n in range(3):
                coefs[place, 3 * m + n] = combine(
                    [TAPS[ii][m] for ii in range(3)], [partial[ii][n] for ii in range(3)]) * (1.0 / 9.0)

    def fix_rows(first, count, work):
        @pl.loop(jnp.maximum(first, 0), jnp.minimum(first + count, TILE))
        def _(row):
            for tile in range(3):
                work(row, tile, 3 * row + tile)

    def fix_cols(first, count, work):
        low = lax.div(jnp.maximum(first, 0), BLOCK)
        high = lax.div(jnp.minimum(first + count, TILE) - 1, BLOCK) + 1

        @pl.loop(low, high)
        def _(tile):
            @pl.loop(0, TILE, unroll=4)
            def _(row):
                work(row, tile, 3 * row + tile)

    def along_ring(work):
        for touches, fixer, first, count in (
            (near_row, fix_rows, -first_k, 1), (far_row, fix_rows, FOOT_X - move_x - first_k, move_x),
            (near_col, fix_cols, -first_l, 1), (far_col, fix_cols, FOOT_Y - move_y - first_l, move_y),
        ):
            @pl.when(touched & touches)
            def _():
                fixer(first, count, work)

    along_ring(weigh)

    @pl.loop(0, CHUNKS)
    def _(chunk):
        wide_nest, wide_parent, arrived = wide_nest_all.at[chunk], wide_parent_all.at[chunk], arrived_all.at[chunk]
        edges, corners, recv_x, recv_y = edges_all.at[chunk], corners_all.at[chunk], recv_x_all.at[chunk], recv_y_all.at[chunk]
        nest_new, parent_new = nest_new_all.at[chunk], parent_new_all.at[chunk]
        fetch(range(6), chunk, lambda copy: copy.wait())

        @pl.loop(0, TILE, unroll=8)
        def _(row):
            nest_new[row] = wide_nest[row + REFINE * move_x, pl.ds(REFINE * move_y, TILE, stride=1), :]

        def blended(row, cols, shifted, interp):
            entered = (cols >= FINE_Y - REFINE * move_y) | (cols * 0 + row >= FINE_X - REFINE * move_x)
            moved = jnp.where(entered, interp, shifted)
            distance = jnp.minimum(jnp.minimum(cols, FINE_Y - 1 - cols), jnp.minimum(row, FINE_X - 1 - row))
            return moved + blend_of(distance) * (interp - moved)

        def edge_columns(at_near):
            rel_row = BLOCK * lax.rem(me_x + q_x, 3) + phase_x + move_x - 1
            columns = iota(BLOCK)
            if at_near:
                first_col, step, bound, base = 0, columns, TILE * (lax.div(q_y, 3) + 1), corner_y - 1
            else:
                first_col, step = TILE - BLOCK, columns - 2
                bound, base = TILE * (lax.div(q_y + NY - 1, 3) + 1), corner_y - 1 + FOOT_Y - 2
            beyond = base + columns >= bound
            cell = jnp.where(step >= 3, 1, 0)
            sub = step - 3 * cell
            taps = []
            for n in range(3 if at_near else 4):
                m = n - cell
                left = jnp.where(m == 0, 1 / 3, jnp.where(m == 1, 2 / 3, 0.0))
                mid = jnp.where(m == 1, 1.0, 0.0)
                right = jnp.where(m == 1, 2 / 3, jnp.where(m == 2, 1 / 3, 0.0))
                taps.append(jnp.where(sub == 0, left, jnp.where(sub == 1, mid, right)))
            in_strip = (step >= 0) & (step < (3 if at_near else 6))
            for m in range(10):
                second = jnp.where(rel_row + m >= TILE, 1, 0)
                merged_y[m] = jnp.where(beyond, recv_y[1, second, m], recv_y[0, second, m])
                total = None
                for n, tap in enumerate(taps):
                    term = tap * jnp.broadcast_to(merged_y[m, n:n + 1, :], (BLOCK, LANES))
                    total = term if total is None else total + term
                fine_y[m] = total

            @pl.loop(0, BLOCK, unroll=4)
            def _(k):
                for ii in range(3):
                    row = REFINE * k + ii
                    interp = combine(TAPS[ii], [fine_y[k + m] for m in range(3)])
                    shifted = wide_nest[row + REFINE * move_x, pl.ds(first_col + REFINE * move_y, BLOCK, stride=1), :]
                    value = blended(TILE * me_x + row, TILE * me_y + first_col + columns, shifted, interp)
                    nest_new[row, pl.ds(first_col, BLOCK), :] = jnp.where(in_strip, value, shifted)

        def edge_rows(at_near):
            rel_col = BLOCK * lax.rem(me_y + q_y, 3) + phase_y + move_y - 1
            second = rel_col + iota(16) >= TILE
            cols = TILE * me_y + iota(TILE)
            if at_near:
                bound, first_row, cells = TILE * (lax.div(q_x, 3) + 1), corner_x - 1, 1
            else:
                bound, first_row, cells = TILE * (lax.div(q_x + NX - 1, 3) + 1), corner_x - 1 + FOOT_X - 2, 2
            for m in range(cells + 2):
                place = jnp.where(first_row + m >= bound, 1, 0)
                merged_x[...] = jnp.where(second, recv_x[place, 1, m], recv_x[place, 0, m])
                for jj in range(3):
                    fine_x[m, pl.ds(jj, BLOCK, stride=REFINE), :] = combine(
                        TAPS[jj], [merged_x[pl.ds(n, BLOCK), :] for n in range(3)])
            for k in range(cells):
                for ii in range(3):
                    row = (0 if at_near else TILE - 3 * cells) + 3 * k + ii
                    interp = combine(TAPS[ii], [fine_x[k + m] for m in range(3)])
                    shifted = wide_nest[row + REFINE * move_x, pl.ds(REFINE * move_y, TILE, stride=1), :]
                    nest_new[row] = blended(TILE * me_x + row, cols, shifted, interp)

        for at_near in (True, False):
            @pl.when(me_y == (0 if at_near else NY - 1))
            def _():
                edge_columns(at_near)
        for at_near in (True, False):
            @pl.when(me_x == (0 if at_near else NX - 1))
            def _():
                edge_rows(at_near)

        store(0, chunk).start()
        fetch(range(6, len(loads)), chunk, lambda copy: copy.wait())

        @pl.when(jnp.logical_not(touched))
        def _():
            parent_new[...] = wide_parent[pl.ds(1, TILE), pl.ds(8, TILE), :]

        @pl.when(touched)
        def _():
            l = first_l + iota(TILE)
            weight = feeds[chunk]

            @pl.loop(0, TILE, unroll=8)
            def _(row):
                k = l * 0 + (first_k + row)
                covered = (l >= 0) & (l < FOOT_Y) & (k >= 0) & (k < FOOT_X)
                usable = covered & (l < FOOT_Y - move_y) & (k < FOOT_X - move_x)
                at = row + BLOCK - phase_x
                slot_x, in_x = lax.div(at, BLOCK), lax.rem(at, BLOCK)
                whole = jnp.where(usable, arrived[slot_x, in_x], 0.0)
                own = wide_parent[row + 1, pl.ds(8, TILE), :]
                placed[row] = whole
                parent_new[row] = jnp.where(covered, own + weight * (whole - own), own)

            @pl.when(near_row | near_col | far_row | far_col)
            def _():
                for row in range(TILE):
                    wide_parent[row + 1, pl.ds(7, 1), :] = edges[3, row:row + 1, :]
                    wide_parent[row + 1, pl.ds(8 + TILE, 1), :] = edges[2, row:row + 1, :]
                for down, row in ((1, 0), (0, TILE + 1)):
                    wide_parent[row, pl.ds(8, TILE), :] = edges[down]
                    wide_parent[row, pl.ds(7, 1), :] = corners[2 * down + 1, 0:1, :]
                    wide_parent[row, pl.ds(8 + TILE, 1), :] = corners[2 * down, 0:1, :]

                def fix(row, tile, place):
                    cols = first_l + BLOCK * tile + iota(BLOCK)
                    k = first_k + row
                    total = placed[row, pl.ds(pl.multiple_of(BLOCK * tile, BLOCK), BLOCK), :]
                    for m in range(3):
                        for n in range(3):
                            total = total + coefs[place, 3 * m + n] * wide_parent[row + m, pl.ds(7 + BLOCK * tile + n, BLOCK, stride=1), :]
                    covered = (cols >= 0) & (cols < FOOT_Y) & (cols * 0 + k >= 0) & (cols * 0 + k < FOOT_X)
                    own = wide_parent[row + 1, pl.ds(pl.multiple_of(8 + BLOCK * tile, BLOCK), BLOCK), :]
                    parent_new[row, pl.ds(pl.multiple_of(BLOCK * tile, BLOCK), BLOCK), :] = jnp.where(
                        covered, own + weight * (total - own), own)

                along_ring(fix)

        store(1, chunk).start()

    @pl.loop(0, CHUNKS)
    def _(chunk):
        store(0, chunk).wait()
        store(1, chunk).wait()


def local(parent_field, nest_field, anchor, displacement, feedback_weight, rim_weight):
    f32, dma = jnp.float32, pltpu.SemaphoreType.DMA
    smem, hbm, vmem = (pl.BlockSpec(memory_space=space) for space in (pltpu.SMEM, pl.ANY, pltpu.VMEM))
    prepared = ((BLOCK, BLOCK), (5, 4, 16), (5, 10, 8), (4, TILE), (4, 8))
    average, send_x, send_y, parent_edges, parent_corners, route = pl.pallas_call(
        prepare_kernel,
        out_shape=(
            *(jax.ShapeDtypeStruct((*dims, CHAN), f32) for dims in prepared), jax.ShapeDtypeStruct((1,), jnp.int32)),
        in_specs=[smem, smem, smem, hbm, hbm],
        out_specs=(*(vmem for _ in prepared), smem),
        scratch_shapes=[
            pltpu.VMEM((CHUNKS, TILE, TILE, LANES), f32), pltpu.VMEM((CHUNKS, TILE, TILE + 2 * PAD, LANES), f32),
            pltpu.VMEM((BLOCK, 9, BLOCK, LANES), f32), dma((2, CHUNKS)),
        ],
        name="prepare",
    )(anchor, displacement, rim_weight, nest_field, parent_field)
    crossed = lax.switch(
        route[0], [variant(v) for v in VARIANTS], anchor, nest_field, parent_edges, parent_corners, average, send_x, send_y)
    shape = jax.ShapeDtypeStruct((TILE, TILE, CHAN), f32)
    chunked = (
        (TILE + MARGIN, TILE + 8), (TILE + 2, TILE + 16), (4, BLOCK, TILE), (4, TILE), (4, 8), (2, 2, 4, 16), (2, 2, 10, 8),
        (TILE, TILE), (TILE, TILE),
    )
    return pl.pallas_call(
        finish_kernel,
        out_shape=(shape, shape),
        in_specs=[smem, smem, smem, vmem, *([hbm] * 10)],
        out_specs=(hbm, hbm),
        scratch_shapes=[
            *(pltpu.VMEM((CHUNKS, *dims, LANES), f32) for dims in chunked),
            pltpu.VMEM((CHUNKS, 1, LANES), f32),
            pltpu.VMEM((TILE, TILE, LANES), f32),
            pltpu.VMEM((3 * TILE, 9, BLOCK, LANES), f32),
            pltpu.VMEM((16, LANES), f32),
            pltpu.VMEM((4, TILE, LANES), f32),
            pltpu.VMEM((10, 8, LANES), f32),
            pltpu.VMEM((10, 8, LANES), f32),
            dma((10, CHUNKS)), dma((2, CHUNKS)),
        ],
        name="finish",
    )(anchor, displacement, rim_weight, feedback_weight, parent_field, nest_field, *crossed)


VARIANTS = tuple(range(32))


def solution(mesh):
    in_specs = (P("px", "py", None), P("px", "py", None), P(), P(), P(), P())
    out_specs = (P("px", "py", None), P("px", "py", None))
    return jax.shard_map(local, mesh=mesh, in_specs=in_specs, out_specs=out_specs, check_vma=False)
```
